32 devices in a mesh: dp: 8 (over y, x, core), seq: 4 (over z).
Axes of the slice: x: 2, y: 2, z: 4, core: 2. Of those that a mesh axis runs over, the one named last changes fastest.
Arguments:
- states: bfloat16 [4096, 1280], P(('dp', 'seq')), parts along dimension 0, may hold values from -90 to 90
- token_kind: int32 [4096], P(('dp', 'seq')), parts along dimension 0, may hold values from 0 to 3
- episode: int32 [4096], P(('dp', 'seq')), parts along dimension 0, may hold values from 0 to 3, never falling along the last dimension, each value on 1 to 384 neighbouring positions
- kind_table: bfloat16 [4, 1280], replicated, may hold values from -3 to 3
- w_qkv: bfloat16 [1280, 3072], replicated, may hold values from -0.15625 to 0.15625
- w_out: bfloat16 [1024, 1280], replicated, may hold values from -0.1875 to 0.1875
Outputs:
- attended: bfloat16 [4096, 1280], P(('dp', 'seq')), parts along dimension 0
The draws below stay inside these ranges and needn't reach their ends.
There are 8 independent parts, one for each index of `dp`. The reference program is written for one: setup_inputs(seed, part) draws one part's arguments, and reference() takes and returns one part's arrays. A program takes and returns all parts, laid end to end along the dimension named above; an argument that names none is the same for every part. Nothing has to cross between parts.
All inputs are finite; a program needn't handle non-finite values.
Results may differ from the reference program's by a relative error of at most 0.0055.
The reference program's roundings to bfloat16 on the way (of `inputs`, `projected` and `heads_out`) count: a program that leaves them out, or rounds other values in their place, can miss the bound.
Values may be sent and summed in bfloat16 or wider, within the bound.
No kernel may reach another device: no remote copies, remote signals or barrier semaphores. Data moves between devices by JAX's collectives and lax.ppermute only.
A program may use at most 128 MiB of HBM per device.

```python
import math
import jax
import jax.numpy as jnp
import numpy as np
from jax import lax

D = 1280
HEADS = 16
HD = 64
TYPES = 4
EPISODES = 4
SEQ = 512


def draw_states(key, part):
    normal_part = jnp.clip(jax.random.normal(key, (SEQ, D), jnp.float32), -6.0, 6.0)
    return normal_part.astype(jnp.bfloat16)


def plant(result, key, smallest, top_value):
    dims = result.shape
    spot = [jax.random.randint(jax.random.fold_in(key, axis), (), 0, dims[axis]) for axis in range(len(dims))]
    result = result.at[tuple(spot)].set(smallest)
    longest = dims.index(max(dims))
    spot[longest] = (spot[longest] + 1) % dims[longest]
    return result.at[tuple(spot)].set(top_value)


def split_up(count, total, limit, slope):
    weights = [(1 << 20) // math.isqrt(grade ** slope) + 1 for grade in range(2, count + 1)]
    surplus, counts = total - limit - (count - 1), [1] * (count - 1)
    while surplus > 0:
        movable = [i for i in range(count - 1) if counts[i] < limit]
        mass, budget = sum([weights[i] for i in movable]), surplus
        for i in movable:
            extra = min(limit - counts[i], max(1, budget * weights[i] // mass), surplus)
            counts[i] = counts[i] + extra
            surplus = surplus - extra
    return np.array([limit] + counts)


def uneven_parts(key, number_of, total, reach, slope):
    if number_of == 2:
        one = jax.random.randint(key, (), max(1, total - reach), min(reach, total - 1) + 1)
        return jnp.stack([one, total - one])
    sizes = jnp.asarray(split_up(number_of, total, reach, slope), jnp.int32)
    twos = (number_of - 1) // 2
    donor, receiver = sizes[1:1 + 2 * twos:2], sizes[2:2 + 2 * twos:2]
    slack = jnp.minimum(donor - 1, reach - receiver)
    moved = jax.random.randint(jax.random.fold_in(key, 1), (twos,), 0, 1 << 20) % (slack + 1)
    sizes = sizes.at[1:1 + 2 * twos:2].set(donor - moved).at[2:2 + 2 * twos:2].set(receiver + moved)
    return sizes[jax.random.permutation(jax.random.fold_in(key, 2), number_of)]


def noise(rng, shape, scale, most, kind=jnp.bfloat16):
    values = jax.random.normal(rng, shape, jnp.float32) * scale
    return jnp.minimum(jnp.maximum(values, -most), most).astype(kind)


def setup_inputs(seed: int = 0, part: int = 0) -> dict:
    seeds = jax.random.split(jax.random.key(seed), 7)
    part_keys = jax.random.split(jax.random.fold_in(seeds[6], part), 7)
    states = draw_states(jax.random.fold_in(jax.random.fold_in(seeds[6], part), 71), part)
    token_kind = plant(jax.random.randint(part_keys[1], (SEQ,), 0, TYPES), jax.random.fold_in(part_keys[1], 1), 0, TYPES - 1).astype(jnp.int32)
    episode = jnp.searchsorted(jnp.cumsum(uneven_parts(part_keys[2], EPISODES, SEQ, SEQ * 3 // 4, 0)), jnp.arange(SEQ), side="right").astype(jnp.int32)
    kind_table = noise(seeds[3], (TYPES, D), 0.5, 3.0)
    w_qkv = noise(seeds[4], (D, 3 * HEADS * HD), D ** -0.5, 0.15625)
    w_out = noise(seeds[5], (HEADS * HD, D), (HEADS * HD) ** -0.5, 0.1875)
    return dict(states=states, token_kind=token_kind, episode=episode, kind_table=kind_table, w_qkv=w_qkv, w_out=w_out)


def reference(states, token_kind, episode, kind_table, w_qkv, w_out):
    inputs = (states.astype(jnp.float32) + kind_table.astype(jnp.float32)[token_kind]).astype(jnp.bfloat16)
    projected = jnp.dot(inputs, w_qkv, preferred_element_type=jnp.float32).astype(jnp.bfloat16)
    inner = HEADS * HD
    queries = projected[:, :inner].reshape(SEQ, HEADS, HD).astype(jnp.float32)
    key_rows = projected[:, inner:2 * inner].reshape(SEQ, HEADS, HD).astype(jnp.float32)
    value_rows = projected[:, 2 * inner:].reshape(SEQ, HEADS, HD).astype(jnp.float32)
    places = jnp.arange(SEQ, dtype=jnp.int32)
    stride = math.gcd(SEQ, 512)
    temper = 1.0 / math.sqrt(HD)

    def block(offset):
        block_q = lax.dynamic_slice_in_dim(queries, offset, stride, 0)
        block_place = lax.dynamic_slice_in_dim(places, offset, stride, 0)
        block_episode = lax.dynamic_slice_in_dim(episode, offset, stride, 0)
        scores = jnp.einsum('qhd,khd->hqk', block_q, key_rows) * temper
        allowed = (places[None, :] <= block_place[:, None]) & (episode[None, :] == block_episode[:, None])
        scores = jnp.where(allowed[None], scores, -1e+30)
        highest = lax.optimization_barrier(jnp.max(scores, axis=2))
        weights = jnp.where(allowed[None], jnp.exp(scores - highest[:, :, None]), 0.0)
        totals = lax.optimization_barrier(jnp.sum(weights, axis=2))
        summed = jnp.einsum('hqk,khd->qhd', weights.astype(jnp.bfloat16).astype(jnp.float32), value_rows)
        return (summed / totals.T[:, :, None]).astype(jnp.bfloat16).reshape(stride, inner)
    offsets = (jnp.arange(SEQ // stride, dtype=jnp.int32) * stride).astype(jnp.int32)
    heads_out = lax.map(block, offsets).reshape(SEQ, inner)
    return jnp.dot(heads_out, w_out, preferred_element_type=jnp.float32).astype(jnp.bfloat16)
```

```python
import functools
import math

import jax
import jax.numpy as jnp
from jax import lax
from jax.experimental import pallas as pl
from jax.experimental.pallas import tpu as pltpu
from jax.sharding import PartitionSpec as P

HEADS = 16
PAIR = 2
CHUNKS = 2
MASKED = -1e30
VMEM = pltpu.VMEM
LIMIT = 40 * 1024 * 1024


def call(body, outs, args, flops, scratch=()):
    moved = sum(a.size * a.dtype.itemsize for a in args)
    return pl.pallas_call(
        body,
        out_shape=outs,
        in_specs=[pl.BlockSpec(memory_space=VMEM)] * len(args),
        out_specs=jax.tree.map(lambda _: pl.BlockSpec(memory_space=VMEM), outs),
        scratch_shapes=list(scratch),
        compiler_params=pltpu.CompilerParams(vmem_limit_bytes=LIMIT),
        cost_estimate=pl.CostEstimate(flops=flops, bytes_accessed=moved, transcendentals=0),
    )(*args)


def shape(dims, dtype):
    return jax.ShapeDtypeStruct(dims, dtype)


def embed_body(states, kinds, table, *outs):
    rows = states.shape[0]
    count = table.shape[0]
    numbers = lax.broadcasted_iota(jnp.int32, (count, rows), 0)
    picked = (numbers == kinds[...]).astype(jnp.bfloat16)
    added = lax.dot_general(
        picked, table[...], (((0,), (0,)), ((), ())), preferred_element_type=jnp.float32
    )
    inputs = (states[...].astype(jnp.float32) + added).astype(jnp.bfloat16)
    size = rows // len(outs)
    for number, out in enumerate(outs):
        out[...] = inputs[number * size : (number + 1) * size]


def fold(first, mask, keys, values_t, wide_q, top, total, acc, factor):
    rows = mask.shape[1]
    head = wide_q.shape[0] // HEADS
    wide_mask = jnp.concatenate([mask] * PAIR, axis=1)
    for pair in range(HEADS // PAIR):
        span = slice(pair * PAIR * head, (pair + 1) * PAIR * head)
        scores = jnp.dot(keys[:, span], wide_q[span, :], preferred_element_type=jnp.float32)
        scores = jnp.where(wide_mask, scores, MASKED)
        here = jnp.max(scores, axis=0, keepdims=True)
        line = slice(pair, pair + 1)
        if first:
            raised = here
        else:
            before = top[line, :]
            raised = jnp.maximum(before, here)
            shrink = jnp.exp2((before - raised) * factor)
        weights = jnp.exp2((scores - raised) * factor)
        added = jnp.sum(weights, axis=0, keepdims=True)
        top[line, :] = raised
        total[line, :] = added if first else total[line, :] * shrink + added
        summed = jnp.dot(
            values_t[span, :], weights.astype(jnp.bfloat16), preferred_element_type=jnp.float32
        )
        for one in range(PAIR):
            place = slice(span.start + one * head, span.start + (one + 1) * head)
            lanes = slice(one * rows, (one + 1) * rows)
            part = summed[one * head : (one + 1) * head, lanes]
            acc[place, :] = part if first else acc[place, :] * shrink[:, lanes] + part


def keys_values(x, w_qkv):
    inner = w_qkv.shape[1] // 3
    keys = jnp.dot(x, w_qkv[:, inner : 2 * inner], preferred_element_type=jnp.float32)
    values = jnp.dot(x, w_qkv[:, 2 * inner :], preferred_element_type=jnp.float32)
    return keys.astype(jnp.bfloat16), values.astype(jnp.bfloat16).T


def own_body(factor, chunks, *refs):
    xs, (ep_row, ep_col, w_qkv), (wide_q, top, total, acc) = (
        refs[:chunks],
        refs[chunks : chunks + 3],
        refs[chunks + 3 :],
    )
    x = jnp.concatenate([r[...] for r in xs], axis=0)
    rows = x.shape[0]
    inner = w_qkv.shape[1] // 3
    head = inner // HEADS
    queries = jnp.dot(x, w_qkv[:, :inner], preferred_element_type=jnp.float32)
    queries = queries.astype(jnp.bfloat16).T
    empty = jnp.zeros((head, rows), jnp.bfloat16)
    for number in range(HEADS):
        one = number % PAIR
        place = slice(number * head, (number + 1) * head)
        parts = [queries[place, :] if k == one else empty for k in range(PAIR)]
        wide_q[place, :] = jnp.concatenate(parts, axis=1)
    keys, values_t = keys_values(x, w_qkv)
    place_k = lax.broadcasted_iota(jnp.int32, (rows, rows), 0)
    place_q = lax.broadcasted_iota(jnp.int32, (rows, rows), 1)
    mask = (place_k <= place_q) & (ep_col[...] == ep_row[...])
    fold(True, mask, keys, values_t, wide_q, top, total, acc, factor)


def step_body(factor, chunks, *refs):
    xs = refs[:chunks]
    ep_row, ep_col, w_qkv, wide_q, top_in, total_in, acc_in, top, total, acc = refs[chunks:]
    x = jnp.concatenate([r[...] for r in xs], axis=0) if chunks > 1 else xs[0][...]
    keys, values_t = keys_values(x, w_qkv)
    mask = ep_col[...] == ep_row[...]
    top[...] = top_in[...]
    total[...] = total_in[...]
    acc[...] = acc_in[...]
    fold(False, mask, keys, values_t, wide_q, top, total, acc, factor)


def finish(total, acc, w_out, out):
    rows = acc.shape[1]
    head = acc.shape[0] // HEADS
    parts = []
    for number in range(HEADS):
        pair, one = divmod(number, PAIR)
        scale = 1.0 / total[pair : pair + 1, one * rows : (one + 1) * rows]
        parts.append((acc[number * head : (number + 1) * head, :] * scale).astype(jnp.bfloat16))
    heads_out = jnp.concatenate(parts, axis=0).T
    out[...] = jnp.dot(heads_out, w_out[...], preferred_element_type=jnp.float32).astype(out.dtype)


def last_body(factor, chunks, *refs):
    w_out, out, top, total, acc = refs[chunks + 7 :]
    step_body(factor, chunks, *refs[: chunks + 7], top, total, acc)
    finish(total, acc, w_out, out)


def local(size, states, token_kind, episode, kind_table, w_qkv, w_out):
    rows, width = states.shape
    inner = w_out.shape[0]
    head = inner // HEADS
    factor = math.log2(math.e) / math.sqrt(head)
    piece = rows // CHUNKS
    xs = call(
        embed_body,
        [shape((piece, width), jnp.bfloat16)] * CHUNKS,
        (states, token_kind.reshape(1, rows), kind_table),
        0,
    )
    known = episode[None]
    reach = 1
    while reach < size:
        pairs = [(i, i + reach) for i in range(size - reach)]
        got = lax.ppermute(known + 1, "seq", pairs) - 1
        known = jnp.concatenate([known, got], axis=0)[:size]
        reach *= 2
    ep_row = episode.reshape(1, rows)
    ep_cols = [known[t].reshape(rows, 1) for t in range(size)]
    f32 = jnp.float32
    state = [
        shape((HEADS // PAIR, PAIR * rows), f32),
        shape((HEADS // PAIR, PAIR * rows), f32),
        shape((inner, rows), f32),
    ]
    unit = 2 * rows * width * inner
    wide_q, *now = call(
        functools.partial(own_body, factor, CHUNKS),
        [shape((inner, PAIR * rows), jnp.bfloat16)] + state,
        (*xs, ep_row, ep_cols[0], w_qkv),
        3 * unit,
    )
    moving = list(xs)
    for hop in range(1, size):
        pairs = [(i, i + 1) for i in range(hop - 1, size - 1)]
        moving = [lax.ppermute(m, "seq", pairs) for m in moving]
        args = (*moving, ep_row, ep_cols[hop], w_qkv, wide_q, *now)
        if hop < size - 1:
            now = call(functools.partial(step_body, factor, CHUNKS), state, args, 2 * unit)
    args = (*args, w_out)
    scratch = [VMEM(s.shape, s.dtype) for s in state]
    return call(
        functools.partial(last_body, factor, CHUNKS),
        shape((rows, w_out.shape[1]), jnp.bfloat16),
        args,
        3 * unit,
        scratch,
    )


def solution(mesh):
    placed = (P(("dp", "seq"), None), P(("dp", "seq")), P(("dp", "seq")), P(), P(), P())
    return jax.shard_map(
        functools.partial(local, mesh.shape["seq"]),
        mesh=mesh,
        in_specs=placed,
        out_specs=P(("dp", "seq"), None),
        check_vma=False,
    )
```

```python
import functools
import math

import jax
import jax.numpy as jnp
from jax import lax
from jax.experimental import pallas as pl
from jax.experimental.pallas import tpu as pltpu
from jax.sharding import PartitionSpec as P

HEADS = 16
PAIR = 2
LINES = HEADS // PAIR
CHUNKS = 2
TILE = 8
MASKED = -1e30
VMEM = pltpu.VMEM
F32 = jnp.float32
BF16 = jnp.bfloat16
LIMIT = 20 * 1024 * 1024


def shape(dims, dtype):
    return jax.ShapeDtypeStruct(dims, dtype)


def call(body, outs, args, cost, scratch=(), aliases=None):
    return pl.pallas_call(
        body,
        out_shape=outs,
        in_specs=[pl.BlockSpec(memory_space=VMEM)] * len(args),
        out_specs=jax.tree.map(lambda _: pl.BlockSpec(memory_space=VMEM), outs),
        scratch_shapes=list(scratch),
        input_output_aliases=aliases or {},
        compiler_params=pltpu.CompilerParams(vmem_limit_bytes=LIMIT),
        cost_estimate=pl.CostEstimate(flops=cost, bytes_accessed=cost // 300, transcendentals=0),
    )(*args)


def pivot_of(size):
    return size // 2 - 1


def roles(size):
    place = lax.axis_index("seq")
    odd = lax.rem(lax.axis_index("dp"), 2) == 1
    return place, odd, odd & (place == pivot_of(size))


def embed_body(states, kinds, episode, table, first, *others):
    rows, width = states.shape
    count = table.shape[0]
    numbers = lax.broadcasted_iota(jnp.int32, (count, rows), 0)
    picked = (numbers == kinds[...]).astype(BF16)
    added = lax.dot_general(
        picked, table[...], (((0,), (0,)), ((), ())), preferred_element_type=F32
    )
    inputs = (states[...].astype(F32) + added).astype(BF16)
    size = rows // (1 + len(others))
    first[:size, :] = inputs[:size]
    first[size:, :] = jnp.zeros((TILE, width), BF16)
    first[size:, :rows] = jnp.broadcast_to(episode[...].astype(F32), (TILE, rows)).astype(BF16)
    for number, out in enumerate(others, 1):
        out[...] = inputs[number * size : (number + 1) * size]


def block_of(refs):
    first = refs[0]
    size = first.shape[0] - TILE
    rows = size * len(refs)
    x = jnp.concatenate([first[:size, :]] + [r[...] for r in refs[1:]], axis=0)
    return x, first[size : size + 1, :rows].astype(F32)


def same_episode(key_episode, query_episode):
    rows = query_episode.shape[1]
    return jnp.broadcast_to(key_episode, (rows, key_episode.shape[1])).T == query_episode


def fold(first, mask, keys, values_t, wide_q, top, total, acc, factor):
    rows = mask.shape[1]
    head = wide_q.shape[0] // HEADS
    wide_mask = jnp.concatenate([mask] * PAIR, axis=1)
    for pair in range(LINES):
        span = slice(pair * PAIR * head, (pair + 1) * PAIR * head)
        scores = jnp.dot(keys[:, span], wide_q[span, :], preferred_element_type=F32)
        scores = jnp.where(wide_mask, scores, MASKED)
        here = jnp.max(scores, axis=0, keepdims=True)
        line = slice(pair, pair + 1)
        if first:
            raised = here
        else:
            before = top[line, :]
            raised = jnp.maximum(before, here)
            shrink = jnp.exp2((before - raised) * factor)
        weights = jnp.exp2((scores - raised) * factor)
        added = jnp.sum(weights, axis=0, keepdims=True)
        top[line, :] = raised
        total[line, :] = added if first else total[line, :] * shrink + added
        summed = jnp.dot(values_t[span, :], weights.astype(BF16), preferred_element_type=F32)
        for one in range(PAIR):
            place = slice(span.start + one * head, span.start + (one + 1) * head)
            lanes = slice(one * rows, (one + 1) * rows)
            part = summed[one * head : (one + 1) * head, lanes]
            acc[place, :] = part if first else acc[place, :] * shrink[:, lanes] + part


def put_keys_values(x, w_qkv, keys, values_t):
    inner = w_qkv.shape[1] // 3
    k = jnp.dot(x, w_qkv[:, inner : 2 * inner], preferred_element_type=F32)
    keys[...] = k.astype(BF16)
    v = jnp.dot(x, w_qkv[:, 2 * inner :], preferred_element_type=F32)
    values_t[...] = v.astype(BF16).T


def put_queries(x, w_qkv, wide_q):
    inner = w_qkv.shape[1] // 3
    head = inner // HEADS
    queries = jnp.dot(x, w_qkv[:, :inner], preferred_element_type=F32).astype(BF16).T
    empty = jnp.zeros((head, x.shape[0]), BF16)
    for number in range(HEADS):
        one = number % PAIR
        place = slice(number * head, (number + 1) * head)
        parts = [queries[place, :] if k == one else empty for k in range(PAIR)]
        wide_q[place, :] = jnp.concatenate(parts, axis=1)


def own_body(factor, *refs):
    xs, w_qkv, (keys, values_t, wide_q, top, total, acc) = refs[:CHUNKS], refs[CHUNKS], refs[-6:]
    x, episode = block_of(xs)
    rows = x.shape[0]
    put_queries(x, w_qkv, wide_q)
    put_keys_values(x, w_qkv, keys, values_t)
    place_k = lax.broadcasted_iota(jnp.int32, (rows, rows), 0)
    place_q = lax.broadcasted_iota(jnp.int32, (rows, rows), 1)
    mask = (place_k <= place_q) & same_episode(episode, episode)
    fold(True, mask, keys, values_t, wide_q, top, total, acc, factor)


def early_body(size, hop, factor, *refs):
    xs, mine = refs[:CHUNKS], refs[CHUNKS]
    w_qkv, wide_q = refs[CHUNKS + 1 : CHUNKS + 3]
    keys, values_t, top, total, acc = refs[-5:]
    place, odd, _ = roles(size)

    @pl.when(odd & (place >= hop) & (place <= pivot_of(size)))
    def _():
        x, episode = block_of(xs)
        put_keys_values(x, w_qkv, keys, values_t)
        mask = same_episode(episode, mine_episode(mine, x.shape[0]))
        fold(False, mask, keys, values_t, wide_q, top, total, acc, factor)


def mine_episode(first, rows):
    size = first.shape[0] - TILE
    return first[size : size + 1, :rows].astype(F32)


def split_three(value):
    high = value.astype(BF16)
    rest = value - high.astype(F32)
    middle = rest.astype(BF16)
    low = (rest - middle.astype(F32)).astype(BF16)
    return [high, middle, low]


def stacked(value):
    rows = value.shape[1] // PAIR
    return jnp.concatenate([value[:, k * rows : (k + 1) * rows] for k in range(PAIR)], axis=0)


def pack(top, total, acc, out):
    inner, rows = acc.shape
    head = inner // HEADS
    scale = 1.0 / total[...]
    for number in range(HEADS):
        pair, one = divmod(number, PAIR)
        place = slice(number * head, (number + 1) * head)
        lanes = slice(one * rows, (one + 1) * rows)
        out[place, :] = (acc[place, :] * scale[pair : pair + 1, lanes]).astype(BF16)
    parts = split_three(stacked(top[...])) + split_three(stacked(total[...]))
    for number, part in enumerate(parts):
        out[inner + number * HEADS : inner + (number + 1) * HEADS, :] = part


def merge(packed, top, total, acc, factor):
    inner, rows = acc.shape
    head = inner // HEADS

    def read(number):
        start = inner + number * 3 * HEADS
        parts = [
            packed[start + k * HEADS : start + (k + 1) * HEADS, :].astype(F32) for k in range(3)
        ]
        whole = (parts[0] + parts[1]) + parts[2]
        return jnp.concatenate([whole[k * LINES : (k + 1) * LINES] for k in range(PAIR)], axis=1)

    other_top, other_total = read(0), read(1)
    before = top[...]
    raised = jnp.maximum(before, other_top)
    shrink = jnp.exp2((before - raised) * factor)
    weight = jnp.exp2((other_top - raised) * factor) * other_total
    top[...] = raised
    total[...] = total[...] * shrink + weight
    for number in range(HEADS):
        pair, one = divmod(number, PAIR)
        place = slice(number * head, (number + 1) * head)
        line, lanes = slice(pair, pair + 1), slice(one * rows, (one + 1) * rows)
        acc[place, :] = (
            acc[place, :] * shrink[line, lanes] + packed[place, :].astype(F32) * weight[line, lanes]
        )


def step_body(size, hop, blocks, factor, *refs):
    refs = list(refs)
    take = lambda count: [refs.pop(0) for _ in range(count)]
    xs, (mine, w_qkv, wide_q) = take(CHUNKS), take(3)
    firsts, kept = take(blocks), take(2 * blocks)
    take(3)
    top, total, acc, keys, values_t, packed = take(6)
    other_q, other_top, other_total, other_acc = take(4)
    place, odd, pivot = roles(size)

    @pl.when(~odd & (place >= hop))
    def _():
        x, episode = block_of(xs)
        put_keys_values(x, w_qkv, keys, values_t)
        mask = same_episode(episode, mine_episode(mine, x.shape[0]))
        fold(False, mask, keys, values_t, wide_q, top, total, acc, factor)

    @pl.when(pivot)
    def _():
        x, episode = block_of(xs)
        put_queries(x, w_qkv, other_q)
        state = (other_q, other_top, other_total, other_acc)
        for number in range(blocks):
            mask = same_episode(mine_episode(firsts[number], x.shape[0]), episode)
            fold(number == 0, mask, *kept[2 * number : 2 * number + 2], *state, factor)
        pack(other_top, other_total, other_acc, packed)
        put_keys_values(x, w_qkv, keys, values_t)


def finish(total, acc, w_out, out):
    inner, rows = acc.shape
    head = inner // HEADS
    parts = []
    for number in range(HEADS):
        pair, one = divmod(number, PAIR)
        scale = 1.0 / total[pair : pair + 1, one * rows : (one + 1) * rows]
        parts.append((acc[number * head : (number + 1) * head, :] * scale).astype(BF16))
    heads_out = jnp.concatenate(parts, axis=0).T
    out[...] = jnp.dot(heads_out, w_out[...], preferred_element_type=F32).astype(out.dtype)


def last_body(size, hops, returns, factor, *refs):
    refs = list(refs)
    take = lambda count: [refs.pop(0) for _ in range(count)]
    xs, (mine, w_qkv, wide_q) = take(CHUNKS), take(3)
    packed = take(returns)
    top_in, total_in, acc_in, w_out, out = take(5)
    top, total, acc, keys, values_t = take(5)
    place, odd, _ = roles(size)
    top[...] = top_in[...]
    total[...] = total_in[...]
    acc[...] = acc_in[...]

    @pl.when(~odd & (place >= hops))
    def _():
        x, episode = block_of(xs)
        put_keys_values(x, w_qkv, keys, values_t)
        mask = same_episode(episode, mine_episode(mine, x.shape[0]))
        fold(False, mask, keys, values_t, wide_q, top, total, acc, factor)

    for number, part in enumerate(packed, 1):

        @pl.when(odd & (place == pivot_of(size) + number))
        def _(part=part):
            merge(part, top, total, acc, factor)

    finish(total, acc, w_out, out)


def local(groups, size, states, token_kind, episode, kind_table, w_qkv, w_out):
    rows, width = states.shape
    inner = w_out.shape[0]
    head = inner // HEADS
    factor = math.log2(math.e) / math.sqrt(head)
    piece = rows // CHUNKS
    pivot = pivot_of(size)
    hops = size - 1
    later = size - 1 - pivot
    even = [g * size for g in range(0, groups, 2)]
    odds = [g * size for g in range(1, groups, 2)]

    def move(value, pairs):
        return lax.ppermute(value, ("dp", "seq"), pairs)

    unit = 2 * rows * width * inner
    chunks = [shape((piece + TILE, width), BF16)] + [shape((piece, width), BF16)] * (CHUNKS - 1)
    mine = call(
        embed_body,
        chunks,
        (states, token_kind.reshape(1, rows), episode.reshape(1, rows), kind_table),
        4 * unit,
    )

    moving = []
    block = mine
    for hop in range(1, size):
        pairs = [(g + i, g + i + 1) for g in even for i in range(hop - 1, size - 1)]
        pairs += [(g + i, g + i - 1) for g in odds for i in range(pivot + 1, size - hop + 1)]
        block = [move(b, pairs) for b in block]
        moving.append(block)
    early = []
    block = mine
    for hop in range(1, pivot + 1):
        pairs = [(g + i, g + i + 1) for g in odds for i in range(hop - 1, pivot)]
        block = [move(b, pairs) for b in block]
        early.append(block)

    state = [
        shape((LINES, PAIR * rows), F32),
        shape((LINES, PAIR * rows), F32),
        shape((inner, rows), F32),
    ]
    wide = shape((inner, PAIR * rows), BF16)
    pair = [shape((rows, inner), BF16), shape((inner, rows), BF16)]
    keys, values_t, wide_q, *now = call(
        functools.partial(own_body, factor), pair + [wide] + state, (*mine, w_qkv), 3 * unit
    )
    firsts, kept = [mine[0]], [keys, values_t]
    for hop, block in enumerate(early, 1):
        args = (*block, mine[0], w_qkv, wide_q, *now)
        keys, values_t, *now = call(
            functools.partial(early_body, size, hop, factor),
            pair + state,
            args,
            2 * unit,
            aliases={len(args) - 3 + k: 2 + k for k in range(3)},
        )
        firsts, kept = firsts + [block[0]], kept + [keys, values_t]
    returned = []
    for hop, block in enumerate(moving[:-1], 1):
        serve = hop <= later
        args = (*block, mine[0], w_qkv, wide_q, *firsts, *kept, *now)
        outs = state + pair + [shape((inner + 6 * HEADS, rows), BF16)]
        *now, keys, values_t, packed = call(
            functools.partial(step_body, size, hop, len(firsts), factor),
            outs,
            args,
            2 * unit,
            [VMEM(s.shape, s.dtype) for s in [wide] + state],
            {len(args) - 3 + k: k for k in range(3)},
        )
        if serve:
            pairs = [(g + pivot, g + pivot + hop) for g in odds]
            returned.append(move(packed, pairs))
        firsts, kept = firsts + [block[0]], kept + [keys, values_t]
    args = (*moving[-1], mine[0], w_qkv, wide_q, *returned, *now, w_out)
    return call(
        functools.partial(last_body, size, hops, len(returned), factor),
        shape((rows, w_out.shape[1]), BF16),
        args,
        3 * unit,
        [VMEM(s.shape, s.dtype) for s in state + pair],
    )


def solution(mesh):
    placed = (P(("dp", "seq"), None), P(("dp", "seq")), P(("dp", "seq")), P(), P(), P())
    return jax.shard_map(
        functools.partial(local, mesh.shape["dp"], mesh.shape["seq"]),
        mesh=mesh,
        in_specs=placed,
        out_specs=P(("dp", "seq"), None),
        check_vma=False,
    )
```

```python
import functools
import math

import jax
import jax.numpy as jnp
from jax import lax
from jax.experimental import pallas as pl
from jax.experimental.pallas import tpu as pltpu
from jax.sharding import PartitionSpec as P

HEADS = 16
PAIR = 2
LINES = HEADS // PAIR
TILE = 8
MASKED = -1e30
VMEM = pltpu.VMEM
HBM = pltpu.HBM
F32 = jnp.float32
BF16 = jnp.bfloat16
LIMIT = 20 * 1024 * 1024


def shape(dims, dtype):
    return jax.ShapeDtypeStruct(dims, dtype)


def call(body, outs, args, cost, scratch=(), aliases=None, spaces=None):
    spaces = spaces or [VMEM] * len(args)
    args = [
        pltpu.with_memory_space_constraint(a, s) if s is HBM else a for a, s in zip(args, spaces)
    ]
    return pl.pallas_call(
        body,
        out_shape=outs,
        in_specs=[pl.BlockSpec(memory_space=s) for s in spaces],
        out_specs=jax.tree.map(lambda _: pl.BlockSpec(memory_space=VMEM), outs),
        scratch_shapes=list(scratch),
        input_output_aliases=aliases or {},
        compiler_params=pltpu.CompilerParams(vmem_limit_bytes=LIMIT),
        cost_estimate=pl.CostEstimate(flops=cost, bytes_accessed=cost // 300, transcendentals=0),
    )(*args)


def plans(size):
    result = []
    for pivot in (size // 2, size // 2 - 1):
        shifts = max(pivot, size - 2 - pivot)
        slots = [("fold", t) for t in range(shifts, 0, -1)]
        slots += [("serve", t) for t in range(1, size - pivot)]
        result.append((pivot, slots))
    return result


def slot_pairs(size, pivot, slot):
    kind, t = slot
    if kind == "serve":
        return [(pivot + t, pivot)]
    return [(i, i + t) for i in range(size - t) if i + t <= pivot or i > pivot]


def receives(size, pivot, slot, place):
    kind, t = slot
    if kind == "serve":
        return place == pivot
    return ((place >= t) & (place <= pivot)) | (place > pivot + t)


def embed_body(states, kinds, episode, table, out, s_in, k_in, e_in, t_in, sems):
    ends = (states, s_in), (kinds, k_in), (episode, e_in), (table, t_in)
    copies = [pltpu.make_async_copy(*end, sems.at[k]) for k, end in enumerate(ends)]
    for copy in copies:
        copy.start()
    for copy in copies[::-1]:
        copy.wait()
    rows, width = states.shape
    count = table.shape[0]
    numbers = lax.broadcasted_iota(jnp.int32, (count, rows), 0)
    picked = (numbers == k_in[...]).astype(BF16)
    added = lax.dot_general(
        picked, t_in[...], (((0,), (0,)), ((), ())), preferred_element_type=F32
    )
    out[:rows, :] = (s_in[...].astype(F32) + added).astype(BF16)
    out[rows:, :] = jnp.zeros((TILE, width), BF16)
    out[rows:, :rows] = jnp.broadcast_to(e_in[...].astype(F32), (TILE, rows)).astype(BF16)


def episode_of(block):
    rows = block.shape[0] - TILE
    return block[rows : rows + 1, :rows].astype(F32)


def same_episode(key_block, query_block):
    keys, queries = episode_of(key_block), episode_of(query_block)
    return jnp.broadcast_to(keys, (queries.shape[1], keys.shape[1])).T == queries


def fold(first, mask, keys, values_t, wide_q, top, total, acc, factor):
    rows = mask.shape[1]
    head = wide_q.shape[0] // HEADS
    wide_mask = jnp.concatenate([mask] * PAIR, axis=1)
    for pair in range(LINES):
        span = slice(pair * PAIR * head, (pair + 1) * PAIR * head)
        scores = jnp.dot(keys[:, span], wide_q[span, :], preferred_element_type=F32)
        scores = jnp.where(wide_mask, scores, MASKED)
        here = jnp.max(scores, axis=0, keepdims=True)
        line = slice(pair, pair + 1)
        if first:
            raised = here
        else:
            before = top[line, :]
            raised = jnp.maximum(before, here)
            shrink = jnp.exp2((before - raised) * factor)
        weights = jnp.exp2((scores - raised) * factor)
        added = jnp.sum(weights, axis=0, keepdims=True)
        top[line, :] = raised
        total[line, :] = added if first else total[line, :] * shrink + added
        summed = jnp.dot(values_t[span, :], weights.astype(BF16), preferred_element_type=F32)
        for one in range(PAIR):
            place = slice(span.start + one * head, span.start + (one + 1) * head)
            lanes = slice(one * rows, (one + 1) * rows)
            part = summed[one * head : (one + 1) * head, lanes]
            acc[place, :] = part if first else acc[place, :] * shrink[:, lanes] + part


def inputs_of(block):
    return block[: block.shape[0] - TILE, :]


def put_keys_values(x, w, keys, values_t):
    inner = w.shape[1] // 3
    keys[...] = jnp.dot(x, w[:, inner : 2 * inner], preferred_element_type=F32).astype(BF16)
    values = jnp.dot(x, w[:, 2 * inner :], preferred_element_type=F32)
    values_t[...] = values.astype(BF16).T


def put_queries(x, w, wide_q):
    inner = w.shape[1] // 3
    head = inner // HEADS
    queries = jnp.dot(x, w[:, :inner], preferred_element_type=F32).astype(BF16).T
    empty = jnp.zeros((head, x.shape[0]), BF16)
    for number in range(HEADS):
        one = number % PAIR
        place = slice(number * head, (number + 1) * head)
        parts = [queries[place, :] if k == one else empty for k in range(PAIR)]
        wide_q[place, :] = jnp.concatenate(parts, axis=1)


def own_body(factor, block, w_qkv, w, keys, values_t, wide_q, top, total, acc, sems):
    inner = w_qkv.shape[1] // 3
    copies = []
    for k in range(3):
        part = (slice(None), slice(k * inner, (k + 1) * inner))
        copies.append(pltpu.make_async_copy(w_qkv.at[part], w.at[part], sems.at[k]))
        copies[k].start()
    x = inputs_of(block)
    rows = x.shape[0]
    copies[0].wait()
    put_queries(x, w, wide_q)
    copies[1].wait()
    copies[2].wait()
    put_keys_values(x, w, keys, values_t)
    place_k = lax.broadcasted_iota(jnp.int32, (rows, rows), 0)
    place_q = lax.broadcasted_iota(jnp.int32, (rows, rows), 1)
    mask = (place_k <= place_q) & same_episode(block, block)
    fold(True, mask, keys, values_t, wide_q, top, total, acc, factor)


def split_three(value):
    high = value.astype(BF16)
    rest = value - high.astype(F32)
    middle = rest.astype(BF16)
    low = (rest - middle.astype(F32)).astype(BF16)
    return [high, middle, low]


def pack(top, total, acc, out):
    inner, rows = acc.shape
    head = inner // HEADS
    scale = 1.0 / total[...]
    for number in range(HEADS):
        pair, one = divmod(number, PAIR)
        place = slice(number * head, (number + 1) * head)
        lanes = slice(one * rows, (one + 1) * rows)
        out[place, :] = (acc[place, :] * scale[pair : pair + 1, lanes]).astype(BF16)
    parts = []
    for value in (top[...], total[...]):
        lanes = [value[:, k * rows : (k + 1) * rows] for k in range(PAIR)]
        parts += split_three(jnp.concatenate(lanes, axis=0))
    for number, part in enumerate(parts):
        out[inner + number * HEADS : inner + (number + 1) * HEADS, :] = part


def merge(packed, top, total, acc, factor):
    inner, rows = acc.shape
    head = inner // HEADS

    def read(number):
        start = inner + number * 3 * HEADS
        parts = [
            packed[start + k * HEADS : start + (k + 1) * HEADS, :].astype(F32) for k in range(3)
        ]
        whole = (parts[0] + parts[1]) + parts[2]
        return jnp.concatenate([whole[k * LINES : (k + 1) * LINES] for k in range(PAIR)], axis=1)

    other_top, other_total = read(0), read(1)
    before = top[...]
    raised = jnp.maximum(before, other_top)
    shrink = jnp.exp2((before - raised) * factor)
    weight = jnp.exp2((other_top - raised) * factor) * other_total
    top[...] = raised
    total[...] = total[...] * shrink + weight
    for number in range(HEADS):
        pair, one = divmod(number, PAIR)
        place = slice(number * head, (number + 1) * head)
        line, lanes = slice(pair, pair + 1), slice(one * rows, (one + 1) * rows)
        acc[place, :] = (
            acc[place, :] * shrink[line, lanes] + packed[place, :].astype(F32) * weight[line, lanes]
        )


def slot_body(size, jobs, kept_at, count, factor, folds, serves, *refs):
    refs = list(refs)
    take = lambda count: [refs.pop(0) for _ in range(count)]
    block, mine, w, wide_q = take(4)
    blocks, kept = take(count), take(2 * count)
    take(3)
    top, total, acc = take(3)
    keys, values_t = take(2) if folds else (None, None)
    packed = take(1)[0] if serves else None
    place = lax.axis_index("seq")
    parity = lax.rem(lax.axis_index("dp"), 2)
    for number, (pivot, slot) in enumerate(jobs):
        if slot is None:
            continue

        @pl.when((parity == number) & receives(size, pivot, slot, place))
        def _(kind=slot[0], numbers=kept_at[number]):
            x = inputs_of(block)
            if kind == "fold":
                put_keys_values(x, w, keys, values_t)
                mask = same_episode(block, mine)
                fold(False, mask, keys, values_t, wide_q, top, total, acc, factor)
            else:
                other_q, *state = refs
                put_queries(x, w, other_q)
                for order, k in enumerate(numbers):
                    mask = same_episode(blocks[k], block)
                    pair = kept[2 * k : 2 * k + 2]
                    fold(order == 0, mask, *pair, other_q, *state, factor)
                pack(*state, packed)


def last_body(targets, factor, *refs):
    count = len(targets)
    packed = refs[:count]
    top_in, total_in, acc_in, w_out, out, top, total, acc = refs[count:]
    place = lax.axis_index("seq")
    parity = lax.rem(lax.axis_index("dp"), 2)
    top[...] = top_in[...]
    total[...] = total_in[...]
    acc[...] = acc_in[...]
    for part, places in zip(packed, targets):
        for number, where in enumerate(places):
            if where is not None:

                @pl.when((parity == number) & (place == where))
                def _(part=part):
                    merge(part, top, total, acc, factor)

    inner, rows = acc.shape
    head = inner // HEADS
    parts = []
    for number in range(HEADS):
        pair, one = divmod(number, PAIR)
        scale = 1.0 / total[pair : pair + 1, one * rows : (one + 1) * rows]
        parts.append((acc[number * head : (number + 1) * head, :] * scale).astype(BF16))
    heads_out = jnp.concatenate(parts, axis=0).T
    out[...] = jnp.dot(heads_out, w_out[...], preferred_element_type=F32).astype(out.dtype)


def local(groups, size, states, token_kind, episode, kind_table, w_qkv, w_out):
    rows, width = states.shape
    inner = w_out.shape[0]
    head = inner // HEADS
    factor = math.log2(math.e) / math.sqrt(head)
    kinds = plans(size)
    slots = max(len(s) for _, s in kinds)

    def move(value, pairs_by_parity):
        pairs = []
        for group in range(groups):
            pairs += [(group * size + a, group * size + b) for a, b in pairs_by_parity[group % 2]]
        return lax.ppermute(value, ("dp", "seq"), pairs)

    unit = 2 * rows * width * inner
    args = (states, token_kind.reshape(1, rows), episode.reshape(1, rows), kind_table)
    mine = call(
        embed_body,
        shape((rows + TILE, width), BF16),
        args,
        unit,
        [VMEM(a.shape, a.dtype) for a in args] + [pltpu.SemaphoreType.DMA((len(args),))],
        spaces=[HBM] * len(args),
    )
    jobs = [[(p, s[k] if k < len(s) else None) for p, s in kinds] for k in range(slots)]
    moving = []
    for job in jobs:
        moving.append(move(mine, [slot_pairs(size, p, s) if s else [] for p, s in job]))

    state = [
        shape((LINES, PAIR * rows), F32),
        shape((LINES, PAIR * rows), F32),
        shape((inner, rows), F32),
    ]
    wide = shape((inner, PAIR * rows), BF16)
    pair = [shape((rows, inner), BF16), shape((inner, rows), BF16)]
    w, keys, values_t, wide_q, *now = call(
        functools.partial(own_body, factor),
        [shape(w_qkv.shape, w_qkv.dtype)] + pair + [wide] + state,
        (mine, w_qkv),
        3 * unit,
        [pltpu.SemaphoreType.DMA((3,))],
        spaces=[VMEM, HBM],
    )
    blocks, kept, kept_at = [mine], [keys, values_t], [[0], [0]]
    returned, targets = [], []
    for job, block in zip(jobs, moving):
        folds = any(s and s[0] == "fold" for _, s in job)
        serves = any(s and s[0] == "serve" for _, s in job)
        args = (block, mine, w, wide_q, *blocks, *kept, *now)
        outs = state + (pair if folds else [])
        outs += [shape((inner + 6 * HEADS, rows), BF16)] if serves else []
        got = call(
            functools.partial(
                slot_body, size, job, [list(k) for k in kept_at], len(blocks), factor, folds, serves
            ),
            outs,
            args,
            2 * unit,
            [VMEM(s.shape, s.dtype) for s in [wide] + state],
            {len(args) - 3 + k: k for k in range(3)},
        )
        now = got[:3]
        if serves:
            chosen = [(p, s[1]) if s and s[0] == "serve" else None for p, s in job]
            returned.append(move(got[-1], [[(c[0], sum(c))] if c else [] for c in chosen]))
            targets.append([sum(c) if c else None for c in chosen])
        if folds:
            for number, (pivot, slot) in enumerate(job):
                if slot and slot[0] == "fold" and slot[1] <= pivot:
                    kept_at[number].append(len(blocks))
            blocks, kept = blocks + [block], kept + list(got[3:5])
    args = (*returned, *now, w_out)
    return call(
        functools.partial(last_body, targets, factor),
        shape((rows, w_out.shape[1]), BF16),
        args,
        2 * unit,
        [VMEM(s.shape, s.dtype) for s in state],
    )


def solution(mesh):
    placed = (P(("dp", "seq"), None), P(("dp", "seq")), P(("dp", "seq")), P(), P(), P())
    return jax.shard_map(
        functools.partial(local, mesh.shape["dp"], mesh.shape["seq"]),
        mesh=mesh,
        in_specs=placed,
        out_specs=P(("dp", "seq"), None),
        check_vma=False,
    )
```

```python
import functools
import math

import jax
import jax.numpy as jnp
from jax import lax
from jax.experimental import pallas as pl
from jax.experimental.pallas import tpu as pltpu
from jax.sharding import PartitionSpec as P

HEADS = 16
PAIR = 2
LINES = HEADS // PAIR
TILE = 8
SPLIT = 2
MASKED = -1e30
VMEM = pltpu.VMEM
HBM = pltpu.HBM
F32 = jnp.float32
BF16 = jnp.bfloat16
LIMIT = 20 * 1024 * 1024


def shape(dims, dtype):
    return jax.ShapeDtypeStruct(dims, dtype)


def call(body, outs, args, cost, scratch=(), aliases=None, spaces=None):
    spaces = spaces or [VMEM] * len(args)
    args = [
        pltpu.with_memory_space_constraint(a, s) if s is HBM else a for a, s in zip(args, spaces)
    ]
    return pl.pallas_call(
        body,
        out_shape=outs,
        in_specs=[pl.BlockSpec(memory_space=s) for s in spaces],
        out_specs=jax.tree.map(lambda _: pl.BlockSpec(memory_space=VMEM), outs),
        scratch_shapes=list(scratch),
        input_output_aliases=aliases or {},
        compiler_params=pltpu.CompilerParams(vmem_limit_bytes=LIMIT),
        cost_estimate=pl.CostEstimate(flops=cost, bytes_accessed=cost // 300, transcendentals=0),
    )(*args)


def plan_of(size, pivot):
    sources = list(range(pivot - 1, -1, -1)) + list(range(size - 1, pivot, -1))
    slots = [[(source, pivot)] for source in sources]
    for i in range(size):
        for j in range(i):
            if i != pivot and (i < pivot or j > pivot):
                free = [s for s in slots if all(j != a and i != b for a, b in s)]
                if free:
                    free[-1].append((j, i))
                else:
                    slots.append([(j, i)])
    sources += [None] * (len(slots) - len(sources))
    return sources, slots


def embed_body(states, kinds, episode, table, out, s_in, k_in, e_in, t_in, sems):
    ends = (states, s_in), (kinds, k_in), (episode, e_in), (table, t_in)
    copies = [pltpu.make_async_copy(*end, sems.at[k]) for k, end in enumerate(ends)]
    for copy in copies:
        copy.start()
    for copy in copies[::-1]:
        copy.wait()
    rows, width = states.shape
    count = table.shape[0]
    numbers = lax.broadcasted_iota(jnp.int32, (count, rows), 0)
    picked = (numbers == k_in[...]).astype(BF16)
    added = lax.dot_general(
        picked, t_in[...], (((0,), (0,)), ((), ())), preferred_element_type=F32
    )
    out[:rows, :] = (s_in[...].astype(F32) + added).astype(BF16)
    out[rows:, :] = jnp.zeros((TILE, width), BF16)
    out[rows:, :rows] = jnp.broadcast_to(e_in[...].astype(F32), (TILE, rows)).astype(BF16)


def episode_of(block):
    rows = block.shape[0] - TILE
    return block[rows : rows + 1, :rows].astype(F32)


def same_episode(key_block, query_block):
    keys, queries = episode_of(key_block), episode_of(query_block)
    return jnp.broadcast_to(keys, (queries.shape[1], keys.shape[1])).T == queries


def fold(first, mask, keys, values_t, wide_q, top, total, acc, factor):
    rows = mask.shape[1]
    head = wide_q.shape[0] // HEADS
    wide_mask = jnp.concatenate([mask] * PAIR, axis=1)
    for pair in range(LINES):
        span = slice(pair * PAIR * head, (pair + 1) * PAIR * head)
        scores = jnp.dot(keys[:, span], wide_q[span, :], preferred_element_type=F32)
        scores = jnp.where(wide_mask, scores, MASKED)
        here = jnp.max(scores, axis=0, keepdims=True)
        line = slice(pair, pair + 1)
        if first:
            raised = here
        else:
            before = top[line, :]
            raised = jnp.maximum(before, here)
            shrink = jnp.exp2((before - raised) * factor)
        weights = jnp.exp2((scores - raised) * factor)
        added = jnp.sum(weights, axis=0, keepdims=True)
        top[line, :] = raised
        total[line, :] = added if first else total[line, :] * shrink + added
        summed = jnp.dot(values_t[span, :], weights.astype(BF16), preferred_element_type=F32)
        for one in range(PAIR):
            place = slice(span.start + one * head, span.start + (one + 1) * head)
            lanes = slice(one * rows, (one + 1) * rows)
            part = summed[one * head : (one + 1) * head, lanes]
            acc[place, :] = part if first else acc[place, :] * shrink[:, lanes] + part


def inputs_of(block):
    return block[: block.shape[0] - TILE, :]


def put_keys_values(x, w, keys, values_t):
    inner = w.shape[1] // 3
    keys[...] = jnp.dot(x, w[:, inner : 2 * inner], preferred_element_type=F32).astype(BF16)
    values = jnp.dot(x, w[:, 2 * inner :], preferred_element_type=F32)
    values_t[...] = values.astype(BF16).T


def put_queries(x, w, wide_q):
    inner = w.shape[1] // 3
    head = inner // HEADS
    queries = jnp.dot(x, w[:, :inner], preferred_element_type=F32).astype(BF16).T
    empty = jnp.zeros((head, x.shape[0]), BF16)
    for number in range(HEADS):
        one = number % PAIR
        place = slice(number * head, (number + 1) * head)
        parts = [queries[place, :] if k == one else empty for k in range(PAIR)]
        wide_q[place, :] = jnp.concatenate(parts, axis=1)


def own_body(factor, block, w_qkv, w, keys, values_t, wide_q, top, total, acc, sems):
    inner = w_qkv.shape[1] // 3
    depth = w_qkv.shape[0] // SPLIT
    copies = []
    for k in range(3):
        for r in range(SPLIT):
            part = (slice(r * depth, (r + 1) * depth), slice(k * inner, (k + 1) * inner))
            sem = sems.at[k * SPLIT + r]
            copies.append(pltpu.make_async_copy(w_qkv.at[part], w.at[part], sem))
            copies[-1].start()
    x = inputs_of(block)
    rows = x.shape[0]
    for copy in copies[:SPLIT]:
        copy.wait()
    put_queries(x, w, wide_q)
    for copy in copies[SPLIT:]:
        copy.wait()
    put_keys_values(x, w, keys, values_t)
    place_k = lax.broadcasted_iota(jnp.int32, (rows, rows), 0)
    place_q = lax.broadcasted_iota(jnp.int32, (rows, rows), 1)
    mask = (place_k <= place_q) & same_episode(block, block)
    fold(True, mask, keys, values_t, wide_q, top, total, acc, factor)


def split_three(value):
    high = value.astype(BF16)
    rest = value - high.astype(F32)
    middle = rest.astype(BF16)
    low = (rest - middle.astype(F32)).astype(BF16)
    return [high, middle, low]


def pack(top, total, acc, out):
    inner, rows = acc.shape
    head = inner // HEADS
    scale = 1.0 / total[...]
    for number in range(HEADS):
        pair, one = divmod(number, PAIR)
        place = slice(number * head, (number + 1) * head)
        lanes = slice(one * rows, (one + 1) * rows)
        out[place, :] = (acc[place, :] * scale[pair : pair + 1, lanes]).astype(BF16)
    parts = []
    for value in (top[...], total[...]):
        lanes = [value[:, k * rows : (k + 1) * rows] for k in range(PAIR)]
        parts += split_three(jnp.concatenate(lanes, axis=0))
    for number, part in enumerate(parts):
        out[inner + number * HEADS : inner + (number + 1) * HEADS, :] = part


def merge(packed, top, total, acc, factor):
    inner, rows = acc.shape
    head = inner // HEADS

    def read(number):
        start = inner + number * 3 * HEADS
        parts = [
            packed[start + k * HEADS : start + (k + 1) * HEADS, :].astype(F32) for k in range(3)
        ]
        whole = (parts[0] + parts[1]) + parts[2]
        return jnp.concatenate([whole[k * LINES : (k + 1) * LINES] for k in range(PAIR)], axis=1)

    other_top, other_total = read(0), read(1)
    before = top[...]
    raised = jnp.maximum(before, other_top)
    shrink = jnp.exp2((before - raised) * factor)
    weight = jnp.exp2((other_top - raised) * factor) * other_total
    top[...] = raised
    total[...] = total[...] * shrink + weight
    for number in range(HEADS):
        pair, one = divmod(number, PAIR)
        place = slice(number * head, (number + 1) * head)
        line, lanes = slice(pair, pair + 1), slice(one * rows, (one + 1) * rows)
        acc[place, :] = (
            acc[place, :] * shrink[line, lanes] + packed[place, :].astype(F32) * weight[line, lanes]
        )


def any_of(place, places):
    found = place < 0
    for one in places:
        found = found | (place == one)
    return found


def slot_body(jobs, kept_at, count, factor, folds, serves, *refs):
    refs = list(refs)
    take = lambda count: [refs.pop(0) for _ in range(count)]
    block, mine, w, wide_q = take(4)
    blocks, kept = take(count), take(2 * count)
    take(3)
    top, total, acc = take(3)
    keys, values_t = take(2) if folds else (None, None)
    packed = take(1)[0] if serves else None
    place = lax.axis_index("seq")
    parity = lax.rem(lax.axis_index("dp"), 2)
    for number, (pivot, source, pairs) in enumerate(jobs):
        here = parity == number
        others = [b for _, b in pairs if b != pivot]

        if others:

            @pl.when(here & any_of(place, others))
            def _():
                put_keys_values(inputs_of(block), w, keys, values_t)
                mask = same_episode(block, mine)
                fold(False, mask, keys, values_t, wide_q, top, total, acc, factor)

        if source is None:
            continue

        @pl.when(here & (place == pivot))
        def _(pivot=pivot, source=source, numbers=kept_at[number]):
            if source < pivot:
                put_keys_values(inputs_of(block), w, keys, values_t)
            else:
                other_q, *state = refs
                put_queries(inputs_of(block), w, other_q)
                for order, k in enumerate(numbers):
                    mask = same_episode(blocks[k], block)
                    pair = kept[2 * k : 2 * k + 2]
                    fold(order == 0, mask, *pair, other_q, *state, factor)
                pack(*state, packed)


def last_body(targets, pivots, kept_at, count, factor, *refs):
    refs = list(refs)
    take = lambda count: [refs.pop(0) for _ in range(count)]
    mine, wide_q = take(2)
    blocks, kept, packed = take(count), take(2 * count), take(len(targets))
    top_in, total_in, acc_in, w_out, out, top, total, acc = refs
    place = lax.axis_index("seq")
    parity = lax.rem(lax.axis_index("dp"), 2)
    top[...] = top_in[...]
    total[...] = total_in[...]
    acc[...] = acc_in[...]
    for number, pivot in enumerate(pivots):

        @pl.when((parity == number) & (place == pivot))
        def _(numbers=kept_at[number]):
            for k in numbers[1:]:
                mask = same_episode(blocks[k], mine)
                pair = kept[2 * k : 2 * k + 2]
                fold(False, mask, *pair, wide_q, top, total, acc, factor)

    for part, places in zip(packed, targets):
        for number, where in enumerate(places):
            if where is not None:

                @pl.when((parity == number) & (place == where))
                def _(part=part):
                    merge(part, top, total, acc, factor)

    inner, rows = acc.shape
    head = inner // HEADS
    parts = []
    for number in range(HEADS):
        pair, one = divmod(number, PAIR)
        scale = 1.0 / total[pair : pair + 1, one * rows : (one + 1) * rows]
        parts.append((acc[number * head : (number + 1) * head, :] * scale).astype(BF16))
    heads_out = jnp.concatenate(parts, axis=0).T
    out[...] = jnp.dot(heads_out, w_out[...], preferred_element_type=F32).astype(out.dtype)


def local(groups, size, states, token_kind, episode, kind_table, w_qkv, w_out):
    rows, width = states.shape
    inner = w_out.shape[0]
    head = inner // HEADS
    factor = math.log2(math.e) / math.sqrt(head)
    pivots = (size // 2, size // 2 - 1)
    kinds = [plan_of(size, pivot) for pivot in pivots]
    count = max(len(sources) for sources, _ in kinds)

    def move(value, pairs_by_parity):
        pairs = []
        for group in range(groups):
            pairs += [(group * size + a, group * size + b) for a, b in pairs_by_parity[group % 2]]
        return lax.ppermute(value, ("dp", "seq"), pairs)

    unit = 2 * rows * width * inner
    args = (states, token_kind.reshape(1, rows), episode.reshape(1, rows), kind_table)
    mine = call(
        embed_body,
        shape((rows + TILE, width), BF16),
        args,
        unit,
        [VMEM(a.shape, a.dtype) for a in args] + [pltpu.SemaphoreType.DMA((len(args),))],
        spaces=[HBM] * len(args),
    )
    jobs = []
    for k in range(count):
        job = []
        for pivot, (sources, slots) in zip(pivots, kinds):
            job.append((pivot, sources[k], slots[k]) if k < len(slots) else (pivot, None, []))
        jobs.append(job)
    moving = [move(mine, [pairs for _, _, pairs in job]) for job in jobs]

    state = [
        shape((LINES, PAIR * rows), F32),
        shape((LINES, PAIR * rows), F32),
        shape((inner, rows), F32),
    ]
    wide = shape((inner, PAIR * rows), BF16)
    pair = [shape((rows, inner), BF16), shape((inner, rows), BF16)]
    w, keys, values_t, wide_q, *now = call(
        functools.partial(own_body, factor),
        [shape(w_qkv.shape, w_qkv.dtype)] + pair + [wide] + state,
        (mine, w_qkv),
        3 * unit,
        [pltpu.SemaphoreType.DMA((3 * SPLIT,))],
        spaces=[VMEM, HBM],
    )
    blocks, kept, kept_at = [mine], [keys, values_t], [[0], [0]]
    returned, targets = [], []
    for job, block in zip(jobs, moving):
        serve = [s if s is not None and s > p else None for p, s, _ in job]
        keep = [s is not None and s < p for p, s, _ in job]
        serves = any(s is not None for s in serve)
        folds = any(keep) or any(b != p for p, _, pairs in job for _, b in pairs)
        args = (block, mine, w, wide_q, *blocks, *kept, *now)
        outs = state + (pair if folds else [])
        outs += [shape((inner + 6 * HEADS, rows), BF16)] if serves else []
        numbers = [list(k) for k in kept_at]
        got = call(
            functools.partial(slot_body, job, numbers, len(blocks), factor, folds, serves),
            outs,
            args,
            2 * unit,
            [VMEM(s.shape, s.dtype) for s in [wide] + state],
            {len(args) - 3 + k: k for k in range(3)},
        )
        now = got[:3]
        if serves:
            pairs = [[] if s is None else [(p, s)] for p, s in zip(pivots, serve)]
            returned.append(move(got[-1], pairs))
            targets.append(serve)
        if any(keep):
            for number in range(len(pivots)):
                if keep[number]:
                    kept_at[number].append(len(blocks))
            blocks, kept = blocks + [block], kept + list(got[3:5])
    args = (mine, wide_q, *blocks, *kept, *returned, *now, w_out)
    return call(
        functools.partial(last_body, targets, pivots, kept_at, len(blocks), factor),
        shape((rows, w_out.shape[1]), BF16),
        args,
        2 * unit,
        [VMEM(s.shape, s.dtype) for s in state],
    )


def solution(mesh):
    placed = (P(("dp", "seq"), None), P(("dp", "seq")), P(("dp", "seq")), P(), P(), P())
    return jax.shard_map(
        functools.partial(local, mesh.shape["dp"], mesh.shape["seq"]),
        mesh=mesh,
        in_specs=placed,
        out_specs=P(("dp", "seq"), None),
        check_vma=False,
    )
```

```python
import functools
import math

import jax
import jax.numpy as jnp
from jax import lax
from jax.experimental import pallas as pl
from jax.experimental.pallas import tpu as pltpu
from jax.sharding import PartitionSpec as P

HEADS = 16
PAIR = 2
LINES = HEADS // PAIR
TILE = 8
SPLIT = 2
MASKED = -1e30
VMEM = pltpu.VMEM
HBM = pltpu.HBM
F32 = jnp.float32
BF16 = jnp.bfloat16
LIMIT = 20 * 1024 * 1024


def shape(dims, dtype):
    return jax.ShapeDtypeStruct(dims, dtype)


def call(body, outs, args, cost, scratch=(), aliases=None, spaces=None):
    spaces = spaces or [VMEM] * len(args)
    args = [
        pltpu.with_memory_space_constraint(a, s) if s is HBM else a for a, s in zip(args, spaces)
    ]
    return pl.pallas_call(
        body,
        out_shape=outs,
        in_specs=[pl.BlockSpec(memory_space=s) for s in spaces],
        out_specs=jax.tree.map(lambda _: pl.BlockSpec(memory_space=VMEM), outs),
        scratch_shapes=list(scratch),
        input_output_aliases=aliases or {},
        compiler_params=pltpu.CompilerParams(vmem_limit_bytes=LIMIT),
        cost_estimate=pl.CostEstimate(flops=cost, bytes_accessed=cost // 300, transcendentals=0),
    )(*args)


def order_of(size, pivot, early):
    keys, queries = list(range(pivot - 1, -1, -1)), list(range(pivot + 1, size))
    if early and keys and queries:
        return keys[:-1] + queries[:1] + keys[-1:] + queries[1:]
    return keys + queries


def embed_body(states, kinds, episode, table, out, s_in, k_in, e_in, t_in, sems):
    ends = (states, s_in), (kinds, k_in), (episode, e_in), (table, t_in)
    copies = [pltpu.make_async_copy(*end, sems.at[k]) for k, end in enumerate(ends)]
    for copy in copies:
        copy.start()
    for copy in copies[::-1]:
        copy.wait()
    rows, width = states.shape
    count = table.shape[0]
    numbers = lax.broadcasted_iota(jnp.int32, (count, rows), 0)
    picked = (numbers == k_in[...]).astype(BF16)
    added = lax.dot_general(
        picked, t_in[...], (((0,), (0,)), ((), ())), preferred_element_type=F32
    )
    out[:rows, :] = (s_in[...].astype(F32) + added).astype(BF16)
    out[rows:, :] = jnp.zeros((TILE, width), BF16)
    out[rows:, :rows] = jnp.broadcast_to(e_in[...].astype(F32), (TILE, rows)).astype(BF16)


def episode_of(block):
    rows = block.shape[0] - TILE
    return block[rows : rows + 1, :rows].astype(F32)


def same_episode(key_block, query_block):
    keys, queries = episode_of(key_block), episode_of(query_block)
    return jnp.broadcast_to(keys, (queries.shape[1], keys.shape[1])).T == queries


def fold(first, mask, keys, values_t, wide_q, top, total, acc, factor):
    rows = mask.shape[1]
    head = wide_q.shape[0] // HEADS
    wide_mask = jnp.concatenate([mask] * PAIR, axis=1)
    for pair in range(LINES):
        span = slice(pair * PAIR * head, (pair + 1) * PAIR * head)
        scores = jnp.dot(keys[:, span], wide_q[span, :], preferred_element_type=F32)
        scores = jnp.where(wide_mask, scores, MASKED)
        here = jnp.max(scores, axis=0, keepdims=True)
        line = slice(pair, pair + 1)
        if first:
            raised = here
        else:
            before = top[line, :]
            raised = jnp.maximum(before, here)
            shrink = jnp.exp2((before - raised) * factor)
        weights = jnp.exp2((scores - raised) * factor)
        added = jnp.sum(weights, axis=0, keepdims=True)
        top[line, :] = raised
        total[line, :] = added if first else total[line, :] * shrink + added
        summed = jnp.dot(values_t[span, :], weights.astype(BF16), preferred_element_type=F32)
        for one in range(PAIR):
            place = slice(span.start + one * head, span.start + (one + 1) * head)
            lanes = slice(one * rows, (one + 1) * rows)
            part = summed[one * head : (one + 1) * head, lanes]
            acc[place, :] = part if first else acc[place, :] * shrink[:, lanes] + part


def inputs_of(block):
    return block[: block.shape[0] - TILE, :]


def put_keys_values(x, w, keys, values_t):
    inner = w.shape[1] // 3
    keys[...] = jnp.dot(x, w[:, inner : 2 * inner], preferred_element_type=F32).astype(BF16)
    values = jnp.dot(x, w[:, 2 * inner :], preferred_element_type=F32)
    values_t[...] = values.astype(BF16).T


def put_queries(x, w, wide_q):
    inner = w.shape[1] // 3
    head = inner // HEADS
    queries = jnp.dot(x, w[:, :inner], preferred_element_type=F32).astype(BF16).T
    empty = jnp.zeros((head, x.shape[0]), BF16)
    for number in range(HEADS):
        one = number % PAIR
        place = slice(number * head, (number + 1) * head)
        parts = [queries[place, :] if k == one else empty for k in range(PAIR)]
        wide_q[place, :] = jnp.concatenate(parts, axis=1)


def own_body(factor, block, w_qkv, again, w, keys, values_t, wide_q, top, total, acc, sems):
    inner = w_qkv.shape[1] // 3
    depth = w_qkv.shape[0] // SPLIT
    copies = []
    for k in range(3):
        for r in range(SPLIT):
            part = (slice(r * depth, (r + 1) * depth), slice(k * inner, (k + 1) * inner))
            sem = sems.at[k * SPLIT + r]
            copies.append(pltpu.make_async_copy(w_qkv.at[part], w.at[part], sem))
            copies[-1].start()
    again[...] = block[...]
    x = inputs_of(block)
    rows = x.shape[0]
    for copy in copies[:SPLIT]:
        copy.wait()
    put_queries(x, w, wide_q)
    for copy in copies[SPLIT:]:
        copy.wait()
    put_keys_values(x, w, keys, values_t)
    place_k = lax.broadcasted_iota(jnp.int32, (rows, rows), 0)
    place_q = lax.broadcasted_iota(jnp.int32, (rows, rows), 1)
    mask = (place_k <= place_q) & same_episode(block, block)
    fold(True, mask, keys, values_t, wide_q, top, total, acc, factor)


def split_three(value):
    high = value.astype(BF16)
    rest = value - high.astype(F32)
    middle = rest.astype(BF16)
    low = (rest - middle.astype(F32)).astype(BF16)
    return [high, middle, low]


def pack(top, total, acc, out):
    inner, rows = acc.shape
    head = inner // HEADS
    scale = 1.0 / total[...]
    for number in range(HEADS):
        pair, one = divmod(number, PAIR)
        place = slice(number * head, (number + 1) * head)
        lanes = slice(one * rows, (one + 1) * rows)
        out[place, :] = (acc[place, :] * scale[pair : pair + 1, lanes]).astype(BF16)
    parts = []
    for value in (top[...], total[...]):
        lanes = [value[:, k * rows : (k + 1) * rows] for k in range(PAIR)]
        parts += split_three(jnp.concatenate(lanes, axis=0))
    for number, part in enumerate(parts):
        out[inner + number * HEADS : inner + (number + 1) * HEADS, :] = part


def merge(packed, top, total, acc, factor):
    inner, rows = acc.shape
    head = inner // HEADS

    def read(number):
        start = inner + number * 3 * HEADS
        parts = [
            packed[start + k * HEADS : start + (k + 1) * HEADS, :].astype(F32) for k in range(3)
        ]
        whole = (parts[0] + parts[1]) + parts[2]
        return jnp.concatenate([whole[k * LINES : (k + 1) * LINES] for k in range(PAIR)], axis=1)

    other_top, other_total = read(0), read(1)
    before = top[...]
    raised = jnp.maximum(before, other_top)
    shrink = jnp.exp2((before - raised) * factor)
    weight = jnp.exp2((other_top - raised) * factor) * other_total
    top[...] = raised
    total[...] = total[...] * shrink + weight
    for number in range(HEADS):
        pair, one = divmod(number, PAIR)
        place = slice(number * head, (number + 1) * head)
        line, lanes = slice(pair, pair + 1), slice(one * rows, (one + 1) * rows)
        acc[place, :] = (
            acc[place, :] * shrink[line, lanes] + packed[place, :].astype(F32) * weight[line, lanes]
        )


def slot_body(jobs, count, factor, *refs):
    refs = list(refs)
    take = lambda count: [refs.pop(0) for _ in range(count)]
    block, w = take(2)
    blocks, kept = take(count), take(2 * count)
    opened = take(5) if any(job["resume"] for job in jobs) else None
    keys, values_t = take(2)
    packed, *state = take(5)
    place = lax.axis_index("seq")
    parity = lax.rem(lax.axis_index("dp"), 2)
    for number, job in enumerate(jobs):
        if job["source"] is None:
            continue

        @pl.when((parity == number) & (place == job["pivot"]))
        def _(job=job):
            if job["source"] < job["pivot"]:
                put_keys_values(inputs_of(block), w, keys, values_t)
                if job["resume"]:
                    queries, other_q, *before = opened
                    for target, value in zip(state[1:], before):
                        target[...] = value[...]
                    mask = same_episode(block, queries)
                    fold(False, mask, keys, values_t, other_q, *state[1:], factor)
                    pack(*state[1:], packed)
            else:
                put_queries(inputs_of(block), w, state[0])
                for order, k in enumerate(job["kept"]):
                    mask = same_episode(blocks[k], block)
                    pair = kept[2 * k : 2 * k + 2]
                    fold(order == 0, mask, *pair, *state, factor)
                if not job["open"]:
                    pack(*state[1:], packed)


def arranged(keeps, sends, opens, jobs, count, factor, *refs):
    resumed = any(job["resume"] for job in jobs)
    start = 2 + 3 * count + (5 if resumed else 0)
    before, after = refs[:start], list(refs[start:])
    sizes, flags = (2, 1, 4), (keeps, sends, opens)
    outs = [[after.pop(0) for _ in range(n)] if flag else None for n, flag in zip(sizes, flags)]
    rest = [o or [after.pop(0) for _ in range(n)] for n, o in zip(sizes, outs)]
    slot_body(jobs, count, factor, *before, *rest[0], *rest[1], *rest[2])


def side_body(size, reach, pivots, factor, *refs):
    block, mine, w, wide_q = refs[:4]
    top, total, acc, keys, values_t = refs[7:]
    place = lax.axis_index("seq")
    parity = lax.rem(lax.axis_index("dp"), 2)
    for number, pivot in enumerate(pivots):
        inside = ((place >= reach) & (place < pivot)) | (place > pivot + reach)

        @pl.when((parity == number) & inside)
        def _():
            put_keys_values(inputs_of(block), w, keys, values_t)
            mask = same_episode(block, mine)
            fold(False, mask, keys, values_t, wide_q, top, total, acc, factor)


def pivot_body(pivots, kept_at, count, factor, *refs):
    refs = list(refs)
    take = lambda count: [refs.pop(0) for _ in range(count)]
    mine, wide_q = take(2)
    blocks, kept = take(count), take(2 * count)
    state = refs[3:]
    place = lax.axis_index("seq")
    parity = lax.rem(lax.axis_index("dp"), 2)
    for number, pivot in enumerate(pivots):

        @pl.when((parity == number) & (place == pivot))
        def _(numbers=kept_at[number]):
            for k in numbers[1:]:
                mask = same_episode(blocks[k], mine)
                fold(False, mask, *kept[2 * k : 2 * k + 2], wide_q, *state, factor)


def last_body(targets, factor, *refs):
    packed = refs[: len(targets)]
    top_in, total_in, acc_in, w_out, out, top, total, acc = refs[len(targets) :]
    place = lax.axis_index("seq")
    parity = lax.rem(lax.axis_index("dp"), 2)
    top[...] = top_in[...]
    total[...] = total_in[...]
    acc[...] = acc_in[...]
    for part, places in zip(packed, targets):
        for number, where in enumerate(places):
            if where is not None:

                @pl.when((parity == number) & (place == where))
                def _(part=part):
                    merge(part, top, total, acc, factor)

    inner, rows = acc.shape
    head = inner // HEADS
    parts = []
    for number in range(HEADS):
        pair, one = divmod(number, PAIR)
        scale = 1.0 / total[pair : pair + 1, one * rows : (one + 1) * rows]
        parts.append((acc[number * head : (number + 1) * head, :] * scale).astype(BF16))
    heads_out = jnp.concatenate(parts, axis=0).T
    out[...] = jnp.dot(heads_out, w_out[...], preferred_element_type=F32).astype(out.dtype)


def local(groups, size, states, token_kind, episode, kind_table, w_qkv, w_out):
    rows, width = states.shape
    inner = w_out.shape[0]
    head = inner // HEADS
    factor = math.log2(math.e) / math.sqrt(head)
    pivots = (size // 2, size // 2 - 1)
    orders = [order_of(size, pivot, number == 0) for number, pivot in enumerate(pivots)]

    def move(value, pairs_by_parity):
        pairs = []
        for group in range(groups):
            pairs += [(group * size + a, group * size + b) for a, b in pairs_by_parity[group % 2]]
        return lax.ppermute(value, ("dp", "seq"), pairs)

    unit = 2 * rows * width * inner
    args = (states, token_kind.reshape(1, rows), episode.reshape(1, rows), kind_table)
    mine = call(
        embed_body,
        shape((rows + TILE, width), BF16),
        args,
        unit,
        [VMEM(a.shape, a.dtype) for a in args] + [pltpu.SemaphoreType.DMA((len(args),))],
        spaces=[HBM] * len(args),
    )
    moving = [
        move(mine, [[(o[k], p)] for o, p in zip(orders, pivots)]) for k in range(size - 1)
    ]

    state = [
        shape((LINES, PAIR * rows), F32),
        shape((LINES, PAIR * rows), F32),
        shape((inner, rows), F32),
    ]
    wide = shape((inner, PAIR * rows), BF16)
    pair = [shape((rows, inner), BF16), shape((inner, rows), BF16)]
    again, w, keys, values_t, wide_q, *now = call(
        functools.partial(own_body, factor),
        [shape(mine.shape, BF16), shape(w_qkv.shape, w_qkv.dtype)] + pair + [wide] + state,
        (mine, w_qkv),
        3 * unit,
        [pltpu.SemaphoreType.DMA((3 * SPLIT,))],
        spaces=[VMEM, HBM],
    )
    blocks, kept, kept_at = [mine], [keys, values_t], [[0], [0]]
    returned, targets, opened = [], [], None
    for k, block in enumerate(moving):
        jobs = []
        for number, (pivot, order) in enumerate(zip(pivots, orders)):
            source = order[k]
            keep = source < pivot
            later_keys = any(one < pivot for one in order[k + 1 :])
            resume = keep and k > 0 and order[k - 1] > pivot
            jobs.append(
                dict(
                    pivot=pivot,
                    source=source,
                    keep=keep,
                    open=not keep and later_keys,
                    resume=resume,
                    returns=order[k - 1] if resume else source if not keep else None,
                    kept=list(kept_at[number]),
                )
            )
            if jobs[-1]["open"]:
                jobs[-1]["returns"] = None
        keeps = any(job["keep"] for job in jobs)
        later = any(one < p for o, p in zip(orders, pivots) for one in o[k:]) and keeps
        serves = [job["returns"] for job in jobs]
        args = (block, w, *blocks, *kept)
        if any(job["resume"] for job in jobs):
            args = (*args, *opened)
        inside = pair
        result = [shape((inner + 6 * HEADS, rows), BF16), wide] + state
        opens = any(job["open"] for job in jobs)
        sends = any(s is not None for s in serves)
        outs = (inside if later else []) + (result[:1] if sends else []) + (result[1:] if opens else [])
        scratch = ([] if later else inside) + ([] if sends else result[:1]) + ([] if opens else result[1:])
        got = list(
            call(
                functools.partial(arranged, later, sends, opens, jobs, len(blocks), factor),
                outs,
                args,
                2 * unit,
                [VMEM(s.shape, s.dtype) for s in scratch],
            )
        )
        made = [got.pop(0) for _ in range(2)] if later else None
        if sends:
            back = [[] if s is None else [(p, s)] for p, s in zip(pivots, serves)]
            returned.append(move(got.pop(0), back))
            targets.append(serves)
        if opens:
            opened = [block, *got]
        if later:
            for number, job in enumerate(jobs):
                if job["keep"]:
                    kept_at[number].append(len(blocks))
            blocks, kept = blocks + [block], kept + made
    for reach in range(1, max(max(p, size - 1 - p) for p in pivots)):
        pairs = [
            [(i, i + reach) for i in range(size - reach) if i + reach < p or i > p] for p in pivots
        ]
        args = (move(again, pairs), mine, w, wide_q, *now)
        now = call(
            functools.partial(side_body, size, reach, pivots, factor),
            state,
            args,
            2 * unit,
            [VMEM(s.shape, s.dtype) for s in pair],
            {4 + k: k for k in range(3)},
        )
    args = (mine, wide_q, *blocks, *kept, *now)
    now = call(
        functools.partial(pivot_body, pivots, kept_at, len(blocks), factor),
        state,
        args,
        unit,
        aliases={len(args) - 3 + k: k for k in range(3)},
    )
    return call(
        functools.partial(last_body, targets, factor),
        shape((rows, w_out.shape[1]), BF16),
        (*returned, *now, w_out),
        2 * unit,
        [VMEM(s.shape, s.dtype) for s in state],
    )


def solution(mesh):
    placed = (P(("dp", "seq"), None), P(("dp", "seq")), P(("dp", "seq")), P(), P(), P())
    return jax.shard_map(
        functools.partial(local, mesh.shape["dp"], mesh.shape["seq"]),
        mesh=mesh,
        in_specs=placed,
        out_specs=P(("dp", "seq"), None),
        check_vma=False,
    )
```

```python
import functools
import math

import jax
import jax.numpy as jnp
from jax import lax
from jax.experimental import pallas as pl
from jax.experimental.pallas import tpu as pltpu
from jax.sharding import PartitionSpec as P

HEADS = 16
PAIR = 2
LINES = HEADS // PAIR
TILE = 8
MASKED = -1e30
VMEM = pltpu.VMEM
HBM = pltpu.HBM
F32 = jnp.float32
BF16 = jnp.bfloat16
LIMIT = 20 * 1024 * 1024


def shape(dims, dtype):
    return jax.ShapeDtypeStruct(dims, dtype)


def call(body, outs, args, cost, scratch=(), aliases=None, spaces=None):
    spaces = spaces or [VMEM] * len(args)
    args = [
        pltpu.with_memory_space_constraint(a, s) if s is HBM else a for a, s in zip(args, spaces)
    ]
    return pl.pallas_call(
        body,
        out_shape=outs,
        in_specs=[pl.BlockSpec(memory_space=s) for s in spaces],
        out_specs=jax.tree.map(lambda _: pl.BlockSpec(memory_space=VMEM), outs),
        scratch_shapes=list(scratch),
        input_output_aliases=aliases or {},
        compiler_params=pltpu.CompilerParams(vmem_limit_bytes=LIMIT),
        cost_estimate=pl.CostEstimate(flops=cost, bytes_accessed=cost // 300, transcendentals=0),
    )(*args)


def order_of(size, pivot, early):
    keys, queries = list(range(pivot - 1, -1, -1)), list(range(pivot + 1, size))
    if early and keys and queries:
        return keys[:-1] + queries[:1] + keys[-1:] + queries[1:]
    return keys + queries


def embed_body(states, kinds, episode, table, out, s_in, k_in, e_in, t_in, sems):
    ends = (states, s_in), (kinds, k_in), (episode, e_in), (table, t_in)
    copies = [pltpu.make_async_copy(*end, sems.at[k]) for k, end in enumerate(ends)]
    for copy in copies:
        copy.start()
    for copy in copies[::-1]:
        copy.wait()
    rows, width = states.shape
    count = table.shape[0]
    numbers = lax.broadcasted_iota(jnp.int32, (count, rows), 0)
    picked = (numbers == k_in[...]).astype(BF16)
    added = lax.dot_general(
        picked, t_in[...], (((0,), (0,)), ((), ())), preferred_element_type=F32
    )
    out[:rows, :] = (s_in[...].astype(F32) + added).astype(BF16)
    out[rows:, :] = jnp.zeros((TILE, width), BF16)
    out[rows:, :rows] = jnp.broadcast_to(e_in[...].astype(F32), (TILE, rows)).astype(BF16)


def episode_of(block):
    rows = block.shape[0] - TILE
    return block[rows : rows + 1, :rows].astype(F32)


def same_episode(key_block, query_block):
    keys, queries = episode_of(key_block), episode_of(query_block)
    return jnp.broadcast_to(keys, (queries.shape[1], keys.shape[1])).T == queries


def fold(first, mask, keys, values_t, wide_q, top, total, acc, factor):
    rows = mask.shape[1]
    head = wide_q.shape[0] // HEADS
    wide_mask = jnp.concatenate([mask] * PAIR, axis=1)
    for pair in range(LINES):
        span = slice(pair * PAIR * head, (pair + 1) * PAIR * head)
        scores = jnp.dot(keys[:, span], wide_q[span, :], preferred_element_type=F32)
        scores = jnp.where(wide_mask, scores, MASKED)
        here = jnp.max(scores, axis=0, keepdims=True)
        line = slice(pair, pair + 1)
        if first:
            raised = here
        else:
            before = top[line, :]
            raised = jnp.maximum(before, here)
            shrink = jnp.exp2((before - raised) * factor)
        weights = jnp.exp2((scores - raised) * factor)
        added = jnp.sum(weights, axis=0, keepdims=True)
        top[line, :] = raised
        total[line, :] = added if first else total[line, :] * shrink + added
        summed = jnp.dot(values_t[span, :], weights.astype(BF16), preferred_element_type=F32)
        for one in range(PAIR):
            place = slice(span.start + one * head, span.start + (one + 1) * head)
            lanes = slice(one * rows, (one + 1) * rows)
            part = summed[one * head : (one + 1) * head, lanes]
            acc[place, :] = part if first else acc[place, :] * shrink[:, lanes] + part


def inputs_of(block):
    return block[: block.shape[0] - TILE, :]


def put_keys_values(x, w, keys, values_t):
    inner = w.shape[1] // 3
    keys[...] = jnp.dot(x, w[:, inner : 2 * inner], preferred_element_type=F32).astype(BF16)
    values = jnp.dot(x, w[:, 2 * inner :], preferred_element_type=F32)
    values_t[...] = values.astype(BF16).T


def put_queries(x, w, wide_q):
    inner = w.shape[1] // 3
    head = inner // HEADS
    queries = jnp.dot(x, w[:, :inner], preferred_element_type=F32).astype(BF16).T
    empty = jnp.zeros((head, x.shape[0]), BF16)
    for number in range(HEADS):
        one = number % PAIR
        place = slice(number * head, (number + 1) * head)
        parts = [queries[place, :] if k == one else empty for k in range(PAIR)]
        wide_q[place, :] = jnp.concatenate(parts, axis=1)


def own_body(factor, block, w, again, keys, values_t, wide_q, top, total, acc):
    again[...] = block[...]
    x = inputs_of(block)
    rows = x.shape[0]
    put_queries(x, w, wide_q)
    put_keys_values(x, w, keys, values_t)
    place_k = lax.broadcasted_iota(jnp.int32, (rows, rows), 0)
    place_q = lax.broadcasted_iota(jnp.int32, (rows, rows), 1)
    mask = (place_k <= place_q) & same_episode(block, block)
    fold(True, mask, keys, values_t, wide_q, top, total, acc, factor)


def split_three(value):
    high = value.astype(BF16)
    rest = value - high.astype(F32)
    middle = rest.astype(BF16)
    low = (rest - middle.astype(F32)).astype(BF16)
    return [high, middle, low]


def pack(top, total, acc, out):
    inner, rows = acc.shape
    head = inner // HEADS
    scale = 1.0 / total[...]
    for number in range(HEADS):
        pair, one = divmod(number, PAIR)
        place = slice(number * head, (number + 1) * head)
        lanes = slice(one * rows, (one + 1) * rows)
        out[place, :] = (acc[place, :] * scale[pair : pair + 1, lanes]).astype(BF16)
    parts = []
    for value in (top[...], total[...]):
        lanes = [value[:, k * rows : (k + 1) * rows] for k in range(PAIR)]
        parts += split_three(jnp.concatenate(lanes, axis=0))
    for number, part in enumerate(parts):
        out[inner + number * HEADS : inner + (number + 1) * HEADS, :] = part


def merge(packed, top, total, acc, factor):
    inner, rows = acc.shape
    head = inner // HEADS

    def read(number):
        start = inner + number * 3 * HEADS
        parts = [
            packed[start + k * HEADS : start + (k + 1) * HEADS, :].astype(F32) for k in range(3)
        ]
        whole = (parts[0] + parts[1]) + parts[2]
        return jnp.concatenate([whole[k * LINES : (k + 1) * LINES] for k in range(PAIR)], axis=1)

    other_top, other_total = read(0), read(1)
    before = top[...]
    raised = jnp.maximum(before, other_top)
    shrink = jnp.exp2((before - raised) * factor)
    weight = jnp.exp2((other_top - raised) * factor) * other_total
    top[...] = raised
    total[...] = total[...] * shrink + weight
    for number in range(HEADS):
        pair, one = divmod(number, PAIR)
        place = slice(number * head, (number + 1) * head)
        line, lanes = slice(pair, pair + 1), slice(one * rows, (one + 1) * rows)
        acc[place, :] = (
            acc[place, :] * shrink[line, lanes] + packed[place, :].astype(F32) * weight[line, lanes]
        )


def slot_body(jobs, count, factor, *refs):
    refs = list(refs)
    take = lambda count: [refs.pop(0) for _ in range(count)]
    block, w = take(2)
    blocks, kept = take(count), take(2 * count)
    opened = take(5) if any(job["resume"] for job in jobs) else None
    keys, values_t = take(2)
    packed, *state = take(5)
    place = lax.axis_index("seq")
    parity = lax.rem(lax.axis_index("dp"), 2)
    for number, job in enumerate(jobs):
        if job["source"] is None:
            continue

        @pl.when((parity == number) & (place == job["pivot"]))
        def _(job=job):
            if job["source"] < job["pivot"]:
                put_keys_values(inputs_of(block), w, keys, values_t)
                if job["resume"]:
                    queries, other_q, *before = opened
                    for target, value in zip(state[1:], before):
                        target[...] = value[...]
                    mask = same_episode(block, queries)
                    fold(False, mask, keys, values_t, other_q, *state[1:], factor)
                    pack(*state[1:], packed)
            else:
                put_queries(inputs_of(block), w, state[0])
                for order, k in enumerate(job["kept"]):
                    mask = same_episode(blocks[k], block)
                    pair = kept[2 * k : 2 * k + 2]
                    fold(order == 0, mask, *pair, *state, factor)
                if not job["open"]:
                    pack(*state[1:], packed)


def arranged(keeps, sends, opens, jobs, count, factor, *refs):
    resumed = any(job["resume"] for job in jobs)
    start = 2 + 3 * count + (5 if resumed else 0)
    before, after = refs[:start], list(refs[start:])
    sizes, flags = (2, 1, 4), (keeps, sends, opens)
    outs = [[after.pop(0) for _ in range(n)] if flag else None for n, flag in zip(sizes, flags)]
    rest = [o or [after.pop(0) for _ in range(n)] for n, o in zip(sizes, outs)]
    slot_body(jobs, count, factor, *before, *rest[0], *rest[1], *rest[2])


def side_body(size, reach, pivots, factor, *refs):
    block, mine, w, wide_q = refs[:4]
    top, total, acc, keys, values_t = refs[7:]
    place = lax.axis_index("seq")
    parity = lax.rem(lax.axis_index("dp"), 2)
    for number, pivot in enumerate(pivots):
        inside = ((place >= reach) & (place < pivot)) | (place > pivot + reach)

        @pl.when((parity == number) & inside)
        def _():
            put_keys_values(inputs_of(block), w, keys, values_t)
            mask = same_episode(block, mine)
            fold(False, mask, keys, values_t, wide_q, top, total, acc, factor)


def pivot_body(pivots, kept_at, count, factor, *refs):
    refs = list(refs)
    take = lambda count: [refs.pop(0) for _ in range(count)]
    mine, wide_q = take(2)
    blocks, kept = take(count), take(2 * count)
    state = refs[3:]
    place = lax.axis_index("seq")
    parity = lax.rem(lax.axis_index("dp"), 2)
    for number, pivot in enumerate(pivots):

        @pl.when((parity == number) & (place == pivot))
        def _(numbers=kept_at[number]):
            for k in numbers[1:]:
                mask = same_episode(blocks[k], mine)
                fold(False, mask, *kept[2 * k : 2 * k + 2], wide_q, *state, factor)


def last_body(targets, factor, *refs):
    packed = refs[: len(targets)]
    top_in, total_in, acc_in, w_out, out, top, total, acc = refs[len(targets) :]
    place = lax.axis_index("seq")
    parity = lax.rem(lax.axis_index("dp"), 2)
    top[...] = top_in[...]
    total[...] = total_in[...]
    acc[...] = acc_in[...]
    for part, places in zip(packed, targets):
        for number, where in enumerate(places):
            if where is not None:

                @pl.when((parity == number) & (place == where))
                def _(part=part):
                    merge(part, top, total, acc, factor)

    inner, rows = acc.shape
    head = inner // HEADS
    parts = []
    for number in range(HEADS):
        pair, one = divmod(number, PAIR)
        scale = 1.0 / total[pair : pair + 1, one * rows : (one + 1) * rows]
        parts.append((acc[number * head : (number + 1) * head, :] * scale).astype(BF16))
    heads_out = jnp.concatenate(parts, axis=0).T
    out[...] = jnp.dot(heads_out, w_out[...], preferred_element_type=F32).astype(out.dtype)


def local(groups, size, states, token_kind, episode, kind_table, w_qkv, w_out):
    rows, width = states.shape
    inner = w_out.shape[0]
    head = inner // HEADS
    factor = math.log2(math.e) / math.sqrt(head)
    pivots = (size // 2, size // 2 - 1)
    orders = [order_of(size, pivot, number == 0) for number, pivot in enumerate(pivots)]

    def move(value, pairs_by_parity):
        pairs = []
        for group in range(groups):
            pairs += [(group * size + a, group * size + b) for a, b in pairs_by_parity[group % 2]]
        return lax.ppermute(value, ("dp", "seq"), pairs)

    unit = 2 * rows * width * inner
    args = (states, token_kind.reshape(1, rows), episode.reshape(1, rows), kind_table)
    mine = call(
        embed_body,
        shape((rows + TILE, width), BF16),
        args,
        30 * unit,
        [VMEM(a.shape, a.dtype) for a in args] + [pltpu.SemaphoreType.DMA((len(args),))],
        spaces=[HBM] * len(args),
    )
    moving = [
        move(mine, [[(o[k], p)] for o, p in zip(orders, pivots)]) for k in range(size - 1)
    ]

    state = [
        shape((LINES, PAIR * rows), F32),
        shape((LINES, PAIR * rows), F32),
        shape((inner, rows), F32),
    ]
    wide = shape((inner, PAIR * rows), BF16)
    pair = [shape((rows, inner), BF16), shape((inner, rows), BF16)]
    again, keys, values_t, wide_q, *now = call(
        functools.partial(own_body, factor),
        [shape(mine.shape, BF16)] + pair + [wide] + state,
        (mine, w_qkv),
        3 * unit,
    )
    blocks, kept, kept_at = [mine], [keys, values_t], [[0], [0]]
    returned, targets, opened = [], [], None
    for k, block in enumerate(moving):
        jobs = []
        for number, (pivot, order) in enumerate(zip(pivots, orders)):
            source = order[k]
            keep = source < pivot
            later_keys = any(one < pivot for one in order[k + 1 :])
            resume = keep and k > 0 and order[k - 1] > pivot
            jobs.append(
                dict(
                    pivot=pivot,
                    source=source,
                    keep=keep,
                    open=not keep and later_keys,
                    resume=resume,
                    returns=order[k - 1] if resume else source if not keep else None,
                    kept=list(kept_at[number]),
                )
            )
            if jobs[-1]["open"]:
                jobs[-1]["returns"] = None
        keeps = any(job["keep"] for job in jobs)
        later = any(one < p for o, p in zip(orders, pivots) for one in o[k:]) and keeps
        serves = [job["returns"] for job in jobs]
        args = (block, w_qkv, *blocks, *kept)
        if any(job["resume"] for job in jobs):
            args = (*args, *opened)
        inside = pair
        result = [shape((inner + 6 * HEADS, rows), BF16), wide] + state
        opens = any(job["open"] for job in jobs)
        sends = any(s is not None for s in serves)
        outs = (inside if later else []) + (result[:1] if sends else []) + (result[1:] if opens else [])
        scratch = ([] if later else inside) + ([] if sends else result[:1]) + ([] if opens else result[1:])
        got = list(
            call(
                functools.partial(arranged, later, sends, opens, jobs, len(blocks), factor),
                outs,
                args,
                2 * unit,
                [VMEM(s.shape, s.dtype) for s in scratch],
            )
        )
        made = [got.pop(0) for _ in range(2)] if later else None
        if sends:
            back = [[] if s is None else [(p, s)] for p, s in zip(pivots, serves)]
            returned.append(move(got.pop(0), back))
            targets.append(serves)
        if opens:
            opened = [block, *got]
        if later:
            for number, job in enumerate(jobs):
                if job["keep"]:
                    kept_at[number].append(len(blocks))
            blocks, kept = blocks + [block], kept + made
    for reach in range(1, max(max(p, size - 1 - p) for p in pivots)):
        pairs = [
            [(i, i + reach) for i in range(size - reach) if i + reach < p or i > p] for p in pivots
        ]
        args = (move(again, pairs), mine, w_qkv, wide_q, *now)
        now = call(
            functools.partial(side_body, size, reach, pivots, factor),
            state,
            args,
            2 * unit,
            [VMEM(s.shape, s.dtype) for s in pair],
            {4 + k: k for k in range(3)},
        )
    args = (mine, wide_q, *blocks, *kept, *now)
    now = call(
        functools.partial(pivot_body, pivots, kept_at, len(blocks), factor),
        state,
        args,
        unit,
        aliases={len(args) - 3 + k: k for k in range(3)},
    )
    return call(
        functools.partial(last_body, targets, factor),
        shape((rows, w_out.shape[1]), BF16),
        (*returned, *now, w_out),
        2 * unit,
        [VMEM(s.shape, s.dtype) for s in state],
    )


def solution(mesh):
    placed = (P(("dp", "seq"), None), P(("dp", "seq")), P(("dp", "seq")), P(), P(), P())
    return jax.shard_map(
        functools.partial(local, mesh.shape["dp"], mesh.shape["seq"]),
        mesh=mesh,
        in_specs=placed,
        out_specs=P(("dp", "seq"), None),
        check_vma=False,
    )
```

```python
import functools
import math

import jax
import jax.numpy as jnp
from jax import lax
from jax.experimental import pallas as pl
from jax.experimental.pallas import tpu as pltpu
from jax.sharding import PartitionSpec as P

HEADS = 16
PAIR = 2
LINES = HEADS // PAIR
TILE = 8
MASKED = -1e30
VMEM = pltpu.VMEM
HBM = pltpu.HBM
F32 = jnp.float32
BF16 = jnp.bfloat16
LIMIT = 20 * 1024 * 1024


def shape(dims, dtype):
    return jax.ShapeDtypeStruct(dims, dtype)


def call(body, outs, args, cost, scratch=(), aliases=None, spaces=None):
    spaces = spaces or [VMEM] * len(args)
    args = [
        pltpu.with_memory_space_constraint(a, s) if s is HBM else a for a, s in zip(args, spaces)
    ]
    return pl.pallas_call(
        body,
        out_shape=outs,
        in_specs=[pl.BlockSpec(memory_space=s) for s in spaces],
        out_specs=jax.tree.map(lambda _: pl.BlockSpec(memory_space=VMEM), outs),
        scratch_shapes=list(scratch),
        input_output_aliases=aliases or {},
        compiler_params=pltpu.CompilerParams(vmem_limit_bytes=LIMIT),
        cost_estimate=pl.CostEstimate(flops=cost, bytes_accessed=cost // 300, transcendentals=0),
    )(*args)


def order_of(size, pivot):
    return list(range(pivot - 1, -1, -1)) + list(range(size - 1, pivot, -1))


def embed_body(states, kinds, episode, table, out, s_in, k_in, e_in, t_in, sems):
    ends = (states, s_in), (kinds, k_in), (episode, e_in), (table, t_in)
    copies = [pltpu.make_async_copy(*end, sems.at[k]) for k, end in enumerate(ends)]
    for copy in copies:
        copy.start()
    for copy in copies[::-1]:
        copy.wait()
    rows, width = states.shape
    count = table.shape[0]
    numbers = lax.broadcasted_iota(jnp.int32, (count, rows), 0)
    picked = (numbers == k_in[...]).astype(BF16)
    added = lax.dot_general(
        picked, t_in[...], (((0,), (0,)), ((), ())), preferred_element_type=F32
    )
    out[:rows, :] = (s_in[...].astype(F32) + added).astype(BF16)
    out[rows:, :] = jnp.zeros((TILE, width), BF16)
    out[rows:, :rows] = jnp.broadcast_to(e_in[...].astype(F32), (TILE, rows)).astype(BF16)


def episode_of(block):
    rows = block.shape[0] - TILE
    return block[rows : rows + 1, :rows].astype(F32)


def same_episode(key_block, query_block):
    keys, queries = episode_of(key_block), episode_of(query_block)
    return jnp.broadcast_to(keys, (queries.shape[1], keys.shape[1])).T == queries


def fold(first, mask, keys, values_t, wide_q, top, total, acc, factor):
    rows = mask.shape[1]
    head = wide_q.shape[0] // HEADS
    wide_mask = jnp.concatenate([mask] * PAIR, axis=1)
    for pair in range(LINES):
        span = slice(pair * PAIR * head, (pair + 1) * PAIR * head)
        scores = jnp.dot(keys[:, span], wide_q[span, :], preferred_element_type=F32)
        scores = jnp.where(wide_mask, scores, MASKED)
        here = jnp.max(scores, axis=0, keepdims=True)
        line = slice(pair, pair + 1)
        if first:
            raised = here
        else:
            before = top[line, :]
            raised = jnp.maximum(before, here)
            shrink = jnp.exp2((before - raised) * factor)
        weights = jnp.exp2((scores - raised) * factor)
        added = jnp.sum(weights, axis=0, keepdims=True)
        top[line, :] = raised
        total[line, :] = added if first else total[line, :] * shrink + added
        summed = jnp.dot(values_t[span, :], weights.astype(BF16), preferred_element_type=F32)
        for one in range(PAIR):
            place = slice(span.start + one * head, span.start + (one + 1) * head)
            lanes = slice(one * rows, (one + 1) * rows)
            part = summed[one * head : (one + 1) * head, lanes]
            acc[place, :] = part if first else acc[place, :] * shrink[:, lanes] + part


def inputs_of(block):
    return block[: block.shape[0] - TILE, :]


def put_keys_values(x, w, keys, values_t):
    inner = w.shape[1] // 3
    keys[...] = jnp.dot(x, w[:, inner : 2 * inner], preferred_element_type=F32).astype(BF16)
    values = jnp.dot(x, w[:, 2 * inner :], preferred_element_type=F32)
    values_t[...] = values.astype(BF16).T


def put_queries(x, w, wide_q):
    inner = w.shape[1] // 3
    head = inner // HEADS
    queries = jnp.dot(x, w[:, :inner], preferred_element_type=F32).astype(BF16).T
    empty = jnp.zeros((head, x.shape[0]), BF16)
    for number in range(HEADS):
        one = number % PAIR
        place = slice(number * head, (number + 1) * head)
        parts = [queries[place, :] if k == one else empty for k in range(PAIR)]
        wide_q[place, :] = jnp.concatenate(parts, axis=1)


def own_body(factor, block, w, again, keys, values_t, wide_q, top, total, acc):
    again[...] = block[...]
    x = inputs_of(block)
    rows = x.shape[0]
    put_queries(x, w, wide_q)
    put_keys_values(x, w, keys, values_t)
    place_k = lax.broadcasted_iota(jnp.int32, (rows, rows), 0)
    place_q = lax.broadcasted_iota(jnp.int32, (rows, rows), 1)
    mask = (place_k <= place_q) & same_episode(block, block)
    fold(True, mask, keys, values_t, wide_q, top, total, acc, factor)


def split_three(value):
    high = value.astype(BF16)
    rest = value - high.astype(F32)
    middle = rest.astype(BF16)
    low = (rest - middle.astype(F32)).astype(BF16)
    return [high, middle, low]


def pack(top, total, acc, out):
    inner, rows = acc.shape
    head = inner // HEADS
    scale = 1.0 / total[...]
    for number in range(HEADS):
        pair, one = divmod(number, PAIR)
        place = slice(number * head, (number + 1) * head)
        lanes = slice(one * rows, (one + 1) * rows)
        out[place, :] = (acc[place, :] * scale[pair : pair + 1, lanes]).astype(BF16)
    parts = []
    for value in (top[...], total[...]):
        lanes = [value[:, k * rows : (k + 1) * rows] for k in range(PAIR)]
        parts += split_three(jnp.concatenate(lanes, axis=0))
    for number, part in enumerate(parts):
        out[inner + number * HEADS : inner + (number + 1) * HEADS, :] = part


def merge(packed, top, total, acc, factor):
    inner, rows = acc.shape
    head = inner // HEADS

    def read(number):
        start = inner + number * 3 * HEADS
        parts = [
            packed[start + k * HEADS : start + (k + 1) * HEADS, :].astype(F32) for k in range(3)
        ]
        whole = (parts[0] + parts[1]) + parts[2]
        return jnp.concatenate([whole[k * LINES : (k + 1) * LINES] for k in range(PAIR)], axis=1)

    other_top, other_total = read(0), read(1)
    before = top[...]
    raised = jnp.maximum(before, other_top)
    shrink = jnp.exp2((before - raised) * factor)
    weight = jnp.exp2((other_top - raised) * factor) * other_total
    top[...] = raised
    total[...] = total[...] * shrink + weight
    for number in range(HEADS):
        pair, one = divmod(number, PAIR)
        place = slice(number * head, (number + 1) * head)
        line, lanes = slice(pair, pair + 1), slice(one * rows, (one + 1) * rows)
        acc[place, :] = (
            acc[place, :] * shrink[line, lanes] + packed[place, :].astype(F32) * weight[line, lanes]
        )


def slot_body(jobs, count, factor, *refs):
    refs = list(refs)
    take = lambda count: [refs.pop(0) for _ in range(count)]
    block, w = take(2)
    blocks, kept = take(count), take(2 * count)
    opened = take(5) if any(job["resume"] for job in jobs) else None
    keys, values_t = take(2)
    packed, *state = take(5)
    place = lax.axis_index("seq")
    parity = lax.rem(lax.axis_index("dp"), 2)
    for number, job in enumerate(jobs):
        if job["source"] is None:
            continue

        @pl.when((parity == number) & (place == job["pivot"]))
        def _(job=job):
            if job["source"] < job["pivot"]:
                put_keys_values(inputs_of(block), w, keys, values_t)
                if job["resume"]:
                    queries, other_q, *before = opened
                    for target, value in zip(state[1:], before):
                        target[...] = value[...]
                    mask = same_episode(block, queries)
                    fold(False, mask, keys, values_t, other_q, *state[1:], factor)
                    pack(*state[1:], packed)
            else:
                put_queries(inputs_of(block), w, state[0])
                for order, k in enumerate(job["kept"]):
                    mask = same_episode(blocks[k], block)
                    pair = kept[2 * k : 2 * k + 2]
                    fold(order == 0, mask, *pair, *state, factor)
                if not job["open"]:
                    pack(*state[1:], packed)


def arranged(keeps, sends, opens, jobs, count, factor, *refs):
    resumed = any(job["resume"] for job in jobs)
    start = 2 + 3 * count + (5 if resumed else 0)
    before, after = refs[:start], list(refs[start:])
    sizes, flags = (2, 1, 4), (keeps, sends, opens)
    outs = [[after.pop(0) for _ in range(n)] if flag else None for n, flag in zip(sizes, flags)]
    rest = [o or [after.pop(0) for _ in range(n)] for n, o in zip(sizes, outs)]
    slot_body(jobs, count, factor, *before, *rest[0], *rest[1], *rest[2])


def side_body(size, reach, pivots, factor, *refs):
    block, mine, w, wide_q = refs[:4]
    top, total, acc, keys, values_t = refs[7:]
    place = lax.axis_index("seq")
    parity = lax.rem(lax.axis_index("dp"), 2)
    for number, pivot in enumerate(pivots):
        inside = ((place >= reach) & (place < pivot)) | (place > pivot + reach)

        @pl.when((parity == number) & inside)
        def _():
            put_keys_values(inputs_of(block), w, keys, values_t)
            mask = same_episode(block, mine)
            fold(False, mask, keys, values_t, wide_q, top, total, acc, factor)


def pivot_body(pivots, kept_at, count, factor, *refs):
    refs = list(refs)
    take = lambda count: [refs.pop(0) for _ in range(count)]
    mine, wide_q = take(2)
    blocks, kept = take(count), take(2 * count)
    state = refs[3:]
    place = lax.axis_index("seq")
    parity = lax.rem(lax.axis_index("dp"), 2)
    for number, pivot in enumerate(pivots):

        @pl.when((parity == number) & (place == pivot))
        def _(numbers=kept_at[number]):
            for k in numbers[1:]:
                mask = same_episode(blocks[k], mine)
                fold(False, mask, *kept[2 * k : 2 * k + 2], wide_q, *state, factor)


def last_body(targets, factor, *refs):
    packed = refs[: len(targets)]
    top_in, total_in, acc_in, w_out, out, top, total, acc = refs[len(targets) :]
    place = lax.axis_index("seq")
    parity = lax.rem(lax.axis_index("dp"), 2)
    top[...] = top_in[...]
    total[...] = total_in[...]
    acc[...] = acc_in[...]
    for part, places in zip(packed, targets):
        for number, where in enumerate(places):
            if where is not None:

                @pl.when((parity == number) & (place == where))
                def _(part=part):
                    merge(part, top, total, acc, factor)

    inner, rows = acc.shape
    head = inner // HEADS
    parts = []
    for number in range(HEADS):
        pair, one = divmod(number, PAIR)
        scale = 1.0 / total[pair : pair + 1, one * rows : (one + 1) * rows]
        parts.append((acc[number * head : (number + 1) * head, :] * scale).astype(BF16))
    heads_out = jnp.concatenate(parts, axis=0).T
    out[...] = jnp.dot(heads_out, w_out[...], preferred_element_type=F32).astype(out.dtype)


def local(groups, size, states, token_kind, episode, kind_table, w_qkv, w_out):
    rows, width = states.shape
    inner = w_out.shape[0]
    head = inner // HEADS
    factor = math.log2(math.e) / math.sqrt(head)
    pivots = (size // 2, size // 2 - 1)
    orders = [order_of(size, pivot) for pivot in pivots]

    def move(value, pairs_by_parity):
        pairs = []
        for group in range(groups):
            pairs += [(group * size + a, group * size + b) for a, b in pairs_by_parity[group % 2]]
        return lax.ppermute(value, ("dp", "seq"), pairs)

    unit = 2 * rows * width * inner
    args = (states, token_kind.reshape(1, rows), episode.reshape(1, rows), kind_table)
    mine = call(
        embed_body,
        shape((rows + TILE, width), BF16),
        args,
        30 * unit,
        [VMEM(a.shape, a.dtype) for a in args] + [pltpu.SemaphoreType.DMA((len(args),))],
        spaces=[HBM] * len(args),
    )
    moving = [
        move(mine, [[(o[k], p)] for o, p in zip(orders, pivots)]) for k in range(size - 1)
    ]

    state = [
        shape((LINES, PAIR * rows), F32),
        shape((LINES, PAIR * rows), F32),
        shape((inner, rows), F32),
    ]
    wide = shape((inner, PAIR * rows), BF16)
    pair = [shape((rows, inner), BF16), shape((inner, rows), BF16)]
    again, keys, values_t, wide_q, *now = call(
        functools.partial(own_body, factor),
        [shape(mine.shape, BF16)] + pair + [wide] + state,
        (mine, w_qkv),
        3 * unit,
    )
    blocks, kept, kept_at = [mine], [keys, values_t], [[0], [0]]
    returned, targets, opened = [], [], None
    for k, block in enumerate(moving):
        jobs = []
        for number, (pivot, order) in enumerate(zip(pivots, orders)):
            source = order[k]
            keep = source < pivot
            later_keys = any(one < pivot for one in order[k + 1 :])
            resume = keep and k > 0 and order[k - 1] > pivot
            jobs.append(
                dict(
                    pivot=pivot,
                    source=source,
                    keep=keep,
                    open=not keep and later_keys,
                    resume=resume,
                    returns=order[k - 1] if resume else source if not keep else None,
                    kept=list(kept_at[number]),
                )
            )
            if jobs[-1]["open"]:
                jobs[-1]["returns"] = None
        keeps = any(job["keep"] for job in jobs)
        later = any(one < p for o, p in zip(orders, pivots) for one in o[k:]) and keeps
        serves = [job["returns"] for job in jobs]
        args = (block, w_qkv, *blocks, *kept)
        if any(job["resume"] for job in jobs):
            args = (*args, *opened)
        inside = pair
        result = [shape((inner + 6 * HEADS, rows), BF16), wide] + state
        opens = any(job["open"] for job in jobs)
        sends = any(s is not None for s in serves)
        outs = (inside if later else []) + (result[:1] if sends else []) + (result[1:] if opens else [])
        scratch = ([] if later else inside) + ([] if sends else result[:1]) + ([] if opens else result[1:])
        got = list(
            call(
                functools.partial(arranged, later, sends, opens, jobs, len(blocks), factor),
                outs,
                args,
                2 * unit,
                [VMEM(s.shape, s.dtype) for s in scratch],
            )
        )
        made = [got.pop(0) for _ in range(2)] if later else None
        if sends:
            back = [[] if s is None else [(p, s)] for p, s in zip(pivots, serves)]
            returned.append(move(got.pop(0), back))
            targets.append(serves)
        if opens:
            opened = [block, *got]
        if later:
            for number, job in enumerate(jobs):
                if job["keep"]:
                    kept_at[number].append(len(blocks))
            blocks, kept = blocks + [block], kept + made
    for reach in range(1, max(max(p, size - 1 - p) for p in pivots)):
        pairs = [
            [(i, i + reach) for i in range(size - reach) if i + reach < p or i > p] for p in pivots
        ]
        args = (move(again, pairs), mine, w_qkv, wide_q, *now)
        now = call(
            functools.partial(side_body, size, reach, pivots, factor),
            state,
            args,
            2 * unit,
            [VMEM(s.shape, s.dtype) for s in pair],
            {4 + k: k for k in range(3)},
        )
    args = (mine, wide_q, *blocks, *kept, *now)
    now = call(
        functools.partial(pivot_body, pivots, kept_at, len(blocks), factor),
        state,
        args,
        unit,
        aliases={len(args) - 3 + k: k for k in range(3)},
    )
    return call(
        functools.partial(last_body, targets, factor),
        shape((rows, w_out.shape[1]), BF16),
        (*returned, *now, w_out),
        2 * unit,
        [VMEM(s.shape, s.dtype) for s in state],
    )


def solution(mesh):
    placed = (P(("dp", "seq"), None), P(("dp", "seq")), P(("dp", "seq")), P(), P(), P())
    return jax.shard_map(
        functools.partial(local, mesh.shape["dp"], mesh.shape["seq"]),
        mesh=mesh,
        in_specs=placed,
        out_specs=P(("dp", "seq"), None),
        check_vma=False,
    )
```
